32 devices in a mesh: dp: 2 (over x), fsdp: 8 (over z, y), seq: 2 (over core).
Axes of the slice: x: 2, y: 2, z: 4, core: 2. Of those that a mesh axis runs over, the one named last changes fastest.
Arguments:
- tokens_in: bfloat16 [16, 1040, 1024], P(('dp', 'fsdp'), 'seq'), may hold values from -6 to 6
- key_mask: int32 [16, 1040], P(('dp', 'fsdp')), may hold values from 0 to 1, as said below
- attn_weights: bfloat16 [2, 1024, 4096], P(None, 'fsdp')
- mlp_weights: bfloat16 [2, 1024, 8192], P(None, 'fsdp')
- vectors: bfloat16 [2, 14, 1024], P(None, None, 'fsdp')
- cotangent: bfloat16 [16, 1040, 1024], P(('dp', 'fsdp'), 'seq'), may hold values from -6 to 6
- first_attn: float32 [2, 1024, 4096], P(None, 'fsdp'), may hold values from -40 to 40
- second_attn: float32 [2, 1024, 4096], P(None, 'fsdp'), may hold values from 0.832 to 8.32
- first_mlp: float32 [2, 1024, 8192], P(None, 'fsdp'), may hold values from -40 to 40
- second_mlp: float32 [2, 1024, 8192], P(None, 'fsdp'), may hold values from 0.832 to 8.32
- first_vec: float32 [2, 14, 1024], P(None, None, 'fsdp'), may hold values from -80 to 80
- second_vec: float32 [2, 14, 1024], P(None, None, 'fsdp'), may hold values from 3.328 to 33.28
Outputs:
- tokens_out: float32 [16, 1040, 1024], P(('dp', 'fsdp'), 'seq')
- grad_tokens: float32 [16, 1040, 1024], P(('dp', 'fsdp'), 'seq')
- grad_attn: float32 [2, 1024, 4096], P(None, 'fsdp')
- grad_mlp: float32 [2, 1024, 8192], P(None, 'fsdp')
- grad_vectors: float32 [2, 14, 1024], P(None, None, 'fsdp')
- step_attn: float32 [2, 1024, 4096], P(None, 'fsdp')
- step_mlp: float32 [2, 1024, 8192], P(None, 'fsdp')
- step_vectors: float32 [2, 14, 1024], P(None, None, 'fsdp')
- new_first_attn: float32 [2, 1024, 4096], P(None, 'fsdp')
- new_second_attn: float32 [2, 1024, 4096], P(None, 'fsdp')
- new_first_mlp: float32 [2, 1024, 8192], P(None, 'fsdp')
- new_second_mlp: float32 [2, 1024, 8192], P(None, 'fsdp')
- new_first_vec: float32 [2, 14, 1024], P(None, None, 'fsdp')
- new_second_vec: float32 [2, 14, 1024], P(None, None, 'fsdp')
The draws below stay inside these ranges and needn't reach their ends.
Inputs may be any that keep to these rules, and one draw needn't show every extreme that they name: `key_mask`: each image's row is 1 on its first slots and 0 on the rest; at least 910 ones and at least one 0 in every row.
All inputs are finite; a program needn't handle non-finite values.
Results may differ from the reference program's by a relative error of at most 0.023.
Values may be sent and summed in bfloat16 or wider, within the bound.
No kernel may reach another device: no remote copies, remote signals or barrier semaphores. Data moves between devices by JAX's collectives and lax.ppermute only.
A program may use at most 320 MiB of HBM per device.

```python
import math
import jax
import jax.numpy as jnp
from jax import lax

D = 1024
H = 16
HD = 64
FF = 4096
L = 2
S = 1040
IMAGES = 16
VROWS = 14


def draw_key_mask(key, part):
    counts = jax.random.randint(key, (IMAGES, 1), S - S // 8, S)
    positions = jnp.arange(S, dtype=jnp.int32)[None, :]
    return (positions < counts).astype(jnp.int32)


def draw_attn_weights(key, part):
    base_draw = jax.random.truncated_normal(key, -3.0, 3.0, (L, D, 4 * D), jnp.float32)
    column = jnp.arange(4 * D)
    factor = jnp.where(column < 3 * D, D ** (-0.5), 8.0 * D ** (-0.5))
    return (base_draw * factor).astype(jnp.bfloat16)


def draw_mlp_weights(key, part):
    base_draw = jax.random.truncated_normal(key, -3.0, 3.0, (L, D, 2 * FF), jnp.float32)
    column = jnp.arange(2 * FF)
    factor = jnp.where(column < FF, D ** (-0.5), 1.5 * FF ** (-0.5))
    return (base_draw * factor).astype(jnp.bfloat16)


def draw_vectors(key, part):
    row_index = jnp.arange(VROWS)[:, None]
    uniform_part = jax.random.uniform(jax.random.fold_in(key, 1), (L, VROWS, D), jnp.float32, 0.5, 1.5)
    normal_part = jax.random.truncated_normal(jax.random.fold_in(key, 2), -3.0, 3.0, (L, VROWS, D), jnp.float32)
    gain_like = (row_index == 0) | (row_index == 5) | (row_index == 6) | (row_index == 9)
    spread = jnp.where(row_index == 3, 0.2, jnp.where(row_index >= 10, 0.5, 0.3))
    return jnp.where(gain_like, uniform_part, spread * normal_part).astype(jnp.bfloat16)


def shard_levels(rng, dims, shards, low, largest):
    def one(axis_at, shards_of):
        heights = jax.random.uniform(jax.random.fold_in(jax.random.fold_in(rng, 6), axis_at), (shards_of,), jnp.float32, low / len(shards), largest / len(shards))
        return jnp.repeat(jnp.exp(heights), dims[axis_at] // shards_of).reshape((-1,) + (1,) * (len(dims) - axis_at - 1))

    loudness = one(*shards[0])
    for cut in shards[1:]:
        loudness = loudness * one(*cut)
    return loudness


def bell_draw(key, extent, deviation, most, shards=(), held_as=jnp.bfloat16):
    values = deviation * jax.random.normal(key, extent, jnp.float32)
    if shards:
        values = values * shard_levels(key, extent, shards, -0.22, 0.18)
    return jnp.clip(values, -most, most).astype(held_as)


def setup_inputs(seed: int = 0) -> dict:
    streams_of = jax.random.split(jax.random.key(seed), 13)
    tokens_in = bell_draw(streams_of[0], (IMAGES, S, D), 1.0, 6.0, ((0, 16), (1, 2)))
    key_mask = draw_key_mask(jax.random.fold_in(streams_of[12], 71), 0)
    attn_weights = draw_attn_weights(jax.random.fold_in(streams_of[12], 71), 0)
    mlp_weights = draw_mlp_weights(jax.random.fold_in(streams_of[12], 71), 0)
    vectors = draw_vectors(jax.random.fold_in(streams_of[12], 71), 0)
    cotangent = bell_draw(streams_of[5], (IMAGES, S, D), 1.0, 6.0, ((0, 16), (1, 2)))
    first_attn = bell_draw(streams_of[6], (L, D, 4 * D), (0.05 * (IMAGES * S) ** 0.5), 40.0, ((1, 8),), jnp.float32)
    second_attn = jnp.clip(jnp.exp(math.log(8.32) - 2.30258504 * jax.random.uniform(streams_of[7], (L, D, 4 * D), jnp.float32) ** shard_levels(streams_of[7], (L, D, 4 * D), ((1, 8),), -0.2, 0.2)), 0.832, 8.32)
    first_mlp = bell_draw(streams_of[8], (L, D, 2 * FF), (0.05 * (IMAGES * S) ** 0.5), 40.0, ((1, 8),), jnp.float32)
    second_mlp = jnp.clip(jnp.exp(math.log(8.32) - 2.30258504 * jax.random.uniform(streams_of[9], (L, D, 2 * FF), jnp.float32) ** shard_levels(streams_of[9], (L, D, 2 * FF), ((1, 8),), -0.2, 0.2)), 0.832, 8.32)
    first_vec = bell_draw(streams_of[10], (L, VROWS, D), (0.1 * (IMAGES * S) ** 0.5), 80.0, ((2, 8),), jnp.float32)
    second_vec = jnp.clip(jnp.exp(math.log(33.28) - 2.30258504 * jax.random.uniform(streams_of[11], (L, VROWS, D), jnp.float32) ** shard_levels(streams_of[11], (L, VROWS, D), ((2, 8),), -0.2, 0.2)), 3.328, 33.28)
    return {"tokens_in": tokens_in, "key_mask": key_mask, "attn_weights": attn_weights, "mlp_weights": mlp_weights, "vectors": vectors, "cotangent": cotangent, "first_attn": first_attn, "second_attn": second_attn, "first_mlp": first_mlp, "second_mlp": second_mlp, "first_vec": first_vec, "second_vec": second_vec}


norm_eps = 1e-06
neg_large = -1e+30
beta_first = 0.9
beta_second = 0.999
adam_eps = 1e-08
decay_rate = 0.05
rate_matrix = 0.01
rate_vector = 0.05
step_count = 10.0
highest = lax.Precision.HIGHEST

@jax.custom_vjp
def low(v):
    return lax.optimization_barrier(v.astype(jnp.bfloat16)).astype(jnp.float32)

@jax.custom_vjp
def low_back(v):
    return v

def low_keep(v):
    return (low(v), None)

def low_pass(kept, grad):
    return (grad,)

def back_keep(v):
    return (v, None)

def back_low(kept, grad):
    return (low(grad),)
low.defvjp(low_keep, low_pass)
low_back.defvjp(back_keep, back_low)

def layer_norm(values, norm_gain, norm_shift):
    center = values - lax.optimization_barrier(jnp.mean(values, axis=-1, keepdims=True))
    spread = lax.optimization_barrier(jnp.mean(center * center, axis=-1, keepdims=True))
    return center * lax.rsqrt(spread + norm_eps) * norm_gain + norm_shift

def attend(pair_set):
    qkv_image, mask_row = pair_set
    query_rows = qkv_image[:, 0]
    key_rows = qkv_image[:, 1]
    value_rows = qkv_image[:, 2]
    scores = jnp.einsum('qhd,khd->hqk', query_rows, key_rows, precision=highest) * HD ** (-0.5)
    scores = jnp.where(mask_row[None, None, :] > 0, scores, neg_large)
    scores = low_back(scores)
    row_top = lax.optimization_barrier(jnp.max(scores, axis=-1, keepdims=True))
    exp_terms = jnp.exp(scores - row_top)
    attention = low(exp_terms / lax.optimization_barrier(jnp.sum(exp_terms, axis=-1, keepdims=True)))
    return jnp.einsum('hqk,khd->qhd', attention, value_rows, precision=highest)

def layer_step(inputs, attn_layer, mlp_layer, vec_rows, mask_rows):
    images = inputs.shape[0]
    normed = low(layer_norm(inputs, vec_rows[0], vec_rows[1]))
    bias_qkv = jnp.concatenate([vec_rows[2], jnp.zeros_like(vec_rows[2]), vec_rows[3]])
    qkv = jnp.einsum('gsd,de->gse', normed, attn_layer[:, :3 * D], precision=highest) + bias_qkv
    qkv = low(low_back(qkv)).reshape(images, S, 3, H, HD)
    mixed_rows = lax.map(jax.checkpoint(attend), (qkv, mask_rows))
    mixed_rows = low(low_back(mixed_rows.reshape(images, S, D)))
    branch = jnp.einsum('gse,de->gsd', mixed_rows, attn_layer[:, 3 * D:], precision=highest) + vec_rows[4]
    branch = low_back(branch)
    middle = inputs + vec_rows[5] * branch
    normed_two = low(layer_norm(middle, vec_rows[6], vec_rows[7]))
    pre_act = jnp.einsum('gsd,df->gsf', normed_two, mlp_layer[:, :FF], precision=highest) + vec_rows[10:].reshape(FF)
    pre_act = low_back(pre_act)
    active = low(jax.nn.gelu(pre_act, approximate=False))
    mlp_out = jnp.einsum('gsf,df->gsd', active, mlp_layer[:, FF:], precision=highest) + vec_rows[8]
    mlp_out = low_back(mlp_out)
    return middle + vec_rows[9] * mlp_out

def forward(inputs, attn_all, mlp_all, vec_all, mask_rows):
    for layer_index in range(L):
        inputs = layer_step(inputs, attn_all[layer_index], mlp_all[layer_index], vec_all[layer_index], mask_rows)
    return inputs

def adam_step(weights, gradient, moment_one, moment_two, step_rate, decay_weight):
    one_new = beta_first * moment_one + (1.0 - beta_first) * gradient
    two_new = beta_second * moment_two + (1.0 - beta_second) * gradient * gradient
    one_hat = one_new / (1.0 - beta_first ** step_count)
    two_hat = two_new / (1.0 - beta_second ** step_count)
    change = -step_rate * (one_hat / (jnp.sqrt(two_hat) + adam_eps) + decay_weight * weights)
    return (change, one_new, two_new)

def reference(tokens_in, key_mask, attn_weights, mlp_weights, vectors, cotangent, first_attn, second_attn, first_mlp, second_mlp, first_vec, second_vec):
    params = (attn_weights.astype(jnp.float32), mlp_weights.astype(jnp.float32), vectors.astype(jnp.float32))
    per_batch = 4
    batches = IMAGES // per_batch
    inputs = tokens_in.astype(jnp.float32).reshape(batches, per_batch, S, D)
    mask_sets = key_mask.reshape(batches, per_batch, S)
    cot_sets = cotangent.astype(jnp.float32).reshape(batches, per_batch, S, D)

    def accumulate(totals, item_set):
        block_in, block_mask, block_cot = item_set

        def run_block(values, attn_all, mlp_all, vec_all):
            return forward(values, attn_all, mlp_all, vec_all, block_mask)
        block_out, pull_back = jax.vjp(run_block, block_in, params[0], params[1], params[2])
        grad_in, grad_a, grad_m, grad_v = pull_back(block_cot)
        return ((totals[0] + grad_a, totals[1] + grad_m, totals[2] + grad_v), (block_out, grad_in))
    zero_set = (jnp.zeros_like(params[0]), jnp.zeros_like(params[1]), jnp.zeros_like(params[2]))
    totals, (block_outs, grads_in) = lax.scan(accumulate, zero_set, (inputs, mask_sets, cot_sets))
    grad_attn, grad_mlp, grad_vectors = totals
    step_attn, one_attn, two_attn = adam_step(params[0], grad_attn, first_attn, second_attn, rate_matrix, decay_rate)
    step_mlp, one_mlp, two_mlp = adam_step(params[1], grad_mlp, first_mlp, second_mlp, rate_matrix, decay_rate)
    step_vectors, one_vec, two_vec = adam_step(params[2], grad_vectors, first_vec, second_vec, rate_vector, 0.0)
    return (block_outs.reshape(IMAGES, S, D), grads_in.reshape(IMAGES, S, D), grad_attn, grad_mlp, grad_vectors, step_attn, step_mlp, step_vectors, one_attn, two_attn, one_mlp, two_mlp, one_vec, two_vec)
```

```python
import functools

import jax
import jax.numpy as jnp
from jax import lax
from jax.experimental import pallas as pl
from jax.experimental.pallas import tpu as pltpu
from jax.sharding import PartitionSpec as P

HD = 64
EPS = 1e-06
B1 = 0.9
B2 = 0.999
ADAM_EPS = 1e-08
DECAY = 0.05
RATE_M = 0.01
RATE_V = 0.05
STEPS = 10.0
ROWS = 14
IZ1, IZ0, IY, IC, IX = range(5)

f32 = jnp.float32
bf16 = jnp.bfloat16
NN = (((1,), (0,)), ((), ()))
NT = (((1,), (1,)), ((), ()))
TN = (((0,), (0,)), ((), ()))
MB = 1 << 20


def dot(a, b, dims=NN):
    return lax.dot_general(a, b, dims, preferred_element_type=f32)


def sds(shape, dtype):
    return jax.ShapeDtypeStruct(shape, dtype)


def call(body, grid, ins, outs, scratch=(), ids=None, us=2, vmem=40, aliases=None, name=None):
    n_pre = 0 if ids is None else 1
    moved = sum(a.size * a.dtype.itemsize for a, s in ins if s.block_shape is not None)
    moved += sum(
        functools.reduce(lambda p, q: p * q, sh, 1) * jnp.dtype(dt).itemsize for sh, dt, _ in outs
    )
    return pl.pallas_call(
        body,
        out_shape=[sds(sh, dt) for sh, dt, _ in outs],
        grid_spec=pltpu.PrefetchScalarGridSpec(
            num_scalar_prefetch=n_pre,
            grid=grid,
            in_specs=[s for _, s in ins],
            out_specs=[s for _, _, s in outs],
            scratch_shapes=list(scratch),
        ),
        compiler_params=pltpu.CompilerParams(vmem_limit_bytes=vmem * MB),
        cost_estimate=pl.CostEstimate(flops=1, bytes_accessed=1, transcendentals=0),
        input_output_aliases=aliases or {},
        name=name,
    )(*(() if ids is None else (ids,)), *[a for a, _ in ins])


def whole(a):
    nd = a.ndim
    return pl.BlockSpec(a.shape, lambda *_: (0,) * nd)


def row_loop(total, fn):
    step = 104 if total % 104 == 0 else 8

    def body(i, carry):
        fn(pl.ds(pl.multiple_of(i * step, 8), step))
        return carry

    lax.fori_loop(0, total // step, body, 0)


def norm_stats(v):
    center = v - jnp.mean(v, axis=-1, keepdims=True)
    rstd = lax.rsqrt(jnp.mean(center * center, axis=-1, keepdims=True) + EPS)
    return center, rstd


def col_sum(v):
    return jnp.sum(v, axis=0, keepdims=True)


def weight_ins(w, rows, nb, index):
    if isinstance(w, tuple):
        spec = pl.BlockSpec((4, rows // 8, nb), lambda k, ids: (0, 0, index(k)))
        return [(p, spec) for p in w]
    return [(w, pl.BlockSpec((rows, nb), lambda k, ids: (0, index(k))))]


def weight_scratch(w, rows, nb):
    return [pltpu.VMEM((rows, nb), bf16)] if isinstance(w, tuple) else []


def weight_ref(ids, refs, spare):
    if len(refs) == 1:
        return refs[0]
    rows = refs[0].shape[1]
    for q in range(4):
        for bit, ref in ((ids[IY], refs[0]), (1 - ids[IY], refs[1])):
            spare[pl.ds(pl.multiple_of((2 * q + bit) * rows, rows), rows), :] = ref[q]
    return spare


def nn_kernel(ids, xo, xt, *rest, n_w, epi, n_extra, n_out, flip):
    w = rest[:n_w]
    extra = rest[n_w : n_w + n_extra]
    outs = rest[n_w + n_extra : n_w + n_extra + n_out]
    xf = rest[n_w + n_extra + n_out]
    half = xo.shape[0]

    @pl.when(pl.program_id(0) == 0)
    def _():
        xf[0:half, :] = xo[...]
        xf[half:, :] = xt[...]
        if flip:
            nb = 256
            for at in range(0, xf.shape[1], nb):
                outs[-1][at : at + nb, :] = xf[:, at : at + nb].T

    w = weight_ref(ids, w, rest[-1])
    epi(ids, dot(xf[...], w[...]), extra, outs)


def nn_call(ids, xo, xt, w, col, steps, nb, epi, extra, outs, name, flip=False, us=5):
    half, width = xo.shape
    outs = list(outs)
    if flip:
        shape = (width, 2 * half)
        outs.append((shape, bf16, pl.BlockSpec(shape, lambda j, ids: (0, 0))))
    wi = weight_ins(w, width, nb, lambda j: col // nb + j)
    body = functools.partial(
        nn_kernel, n_w=len(wi), epi=epi, n_extra=len(extra), n_out=len(outs), flip=flip
    )
    return call(
        body,
        (steps,),
        [(xo, whole(xo)), (xt, whole(xt))] + wi + extra,
        outs,
        [pltpu.VMEM((2 * half, width), bf16)] + weight_scratch(w, width, nb),
        ids=ids,
        us=us,
        name=name,
    )


def epi_qkv(ids, y, extra, outs, *, base):
    (vec,) = extra
    j = pl.program_id(0)
    nb = y.shape[1]
    at = pl.multiple_of(ids[IC] * nb, nb)
    qb = vec[base + 2 : base + 3, pl.ds(at, nb)]
    vb = vec[base + 3 : base + 4, pl.ds(at, nb)]
    bias = jnp.where(j == 0, qb, jnp.where(j == 2, vb, 0.0))
    scale = jnp.where(j == 0, HD ** (-0.5), 1.0)
    outs[0][...] = ((y + bias) * scale).astype(bf16)


def gelu_parts(t):
    a = jnp.abs(t)
    k = 1.0 / (1.0 + 0.23164189 * a)
    e = jnp.exp(-0.5 * t * t)
    poly = k * (
        0.127414796 + k * (-0.142248368 + k * (0.7107068705 + k * (-0.7265760135 + k * 0.5307027145)))
    )
    tail = poly * e
    phi = jnp.where(t < 0, tail, 1.0 - tail)
    return phi, e * 0.3989422804014327


def epi_up(ids, y, extra, outs, *, base, own):
    (vec,) = extra
    j = pl.program_id(0)
    nb = y.shape[1]
    half = ids[IX] if own else 1 - ids[IX]
    row = base + 10 + 2 * ids[IC] + half
    bias = vec[pl.ds(row, 1), pl.ds(pl.multiple_of(j * nb, nb), nb)]
    u = y + bias
    phi, dens = gelu_parts(u)
    outs[0][...] = (u * phi).astype(bf16)
    outs[1][...] = (phi + u * dens).astype(bf16)


def epi_dact(ids, y, extra, outs):
    (gp,) = extra
    du = (y * gp[...].astype(f32)).astype(bf16)
    outs[0][...] = du
    outs[1][...] = col_sum(du.astype(f32))


def epi_plain(ids, y, extra, outs):
    outs[0][...] = y.astype(bf16)


def nt_kernel(ids, *rest, n_ws, epi, n_extra, n_out):
    n_in = sum(1 + n for n in n_ws)
    extra = rest[n_in : n_in + n_extra]
    outs = rest[n_in + n_extra : n_in + n_extra + n_out]
    acc = rest[n_in + n_extra + n_out]
    spares = rest[n_in + n_extra + n_out + 1 :]
    k = pl.program_id(0)
    nb = 256
    pairs = []
    at = 0
    for gi, n in enumerate(n_ws):
        spare = spares[gi] if spares else None
        pairs.append((rest[at], weight_ref(ids, rest[at + 1 : at + 1 + n], spare)))
        at += 1 + n

    def body(i, carry):
        cols = pl.ds(pl.multiple_of(i * nb, nb), nb)
        y = None
        for x, w in pairs:
            xv = x[...]
            v = dot(xv.reshape(xv.shape[-2:]), w[cols, :], NT)
            y = v if y is None else y + v

        @pl.when(k == 0)
        def _():
            acc[:, cols] = y

        @pl.when(k > 0)
        def _():
            acc[:, cols] += y

        return carry

    lax.fori_loop(0, acc.shape[1] // nb, body, 0)

    @pl.when(k == pl.num_programs(0) - 1)
    def _():
        epi(acc, extra, outs)


def nt_call(ids, groups, steps, kb, rows, wide, epi, extra, outs, name):
    ins, n_ws, scratch = [], [], [pltpu.VMEM((rows, wide), f32)]
    for x, xs, w, col in groups:
        ins.append((x, xs))
        wi = weight_ins(w, wide, kb, lambda k, c=col // kb: c + k)
        ins += wi
        n_ws.append(len(wi))
        scratch += weight_scratch(w, wide, kb)
    body = functools.partial(
        nt_kernel, n_ws=tuple(n_ws), epi=epi, n_extra=len(extra), n_out=len(outs)
    )
    return call(body, (steps,), ins + extra, outs, scratch, ids=ids, us=6, name=name)


def epi_send(acc, extra, outs):
    row_loop(acc.shape[0], lambda r: outs[0].__setitem__((r, slice(None)), acc[r, :].astype(bf16)))


def epi_proj(acc, extra, outs, *, base):
    recv, res, vec = extra
    mid_ref, branch_ref, h_ref = outs

    def fn(r):
        branch = acc[r, :] + recv[r, :].astype(f32) + vec[base + 4 : base + 5, :]
        mid = res[r, :].astype(f32) + vec[base + 5 : base + 6, :] * branch
        mid_ref[r, :] = mid
        branch_ref[r, :] = branch.astype(bf16)
        center, rstd = norm_stats(mid)
        h_ref[r, :] = (
            center * rstd * vec[base + 6 : base + 7, :] + vec[base + 7 : base + 8, :]
        ).astype(bf16)

    row_loop(acc.shape[0], fn)


def epi_down(acc, extra, outs, *, base, nxt):
    recv, mid, vec = extra
    out_ref, down_ref, h_ref = outs

    def fn(r):
        down = acc[r, :] + recv[r, :].astype(f32) + vec[base + 8 : base + 9, :]
        down_ref[r, :] = down.astype(bf16)
        res = mid[r, :] + vec[base + 9 : base + 10, :] * down
        out_ref[r, :] = res
        center, rstd = norm_stats(res)
        h_ref[r, :] = (
            center * rstd * vec[nxt : nxt + 1, :] + vec[nxt + 1 : nxt + 2, :]
        ).astype(bf16)

    row_loop(acc.shape[0], fn)


def epi_down_last(acc, extra, outs, *, base):
    recv, mid, vec, cot = extra
    out_ref, dd_ref, sums = outs
    sums[...] = jnp.zeros_like(sums)

    def fn(r):
        down = acc[r, :] + recv[r, :].astype(f32) + vec[base + 8 : base + 9, :]
        scale = vec[base + 9 : base + 10, :]
        out_ref[r, :] = mid[r, :] + scale * down
        g = cot[r, :].astype(f32)
        dd = (g * scale).astype(bf16)
        dd_ref[r, :] = dd
        sums[0:1, :] += col_sum(g * down)
        sums[1:2, :] += col_sum(dd.astype(f32))

    row_loop(acc.shape[0], fn)


def norm_back(grad, values, gain):
    center, rstd = norm_stats(values)
    n = center * rstd
    e = grad * gain
    me = jnp.mean(e, axis=-1, keepdims=True)
    men = jnp.mean(e * n, axis=-1, keepdims=True)
    return n, rstd * (e - me - n * men)


def epi_dh2(acc, extra, outs, *, base):
    recv, mid, g_in, branch, vec = extra
    dm_ref, db_ref, sums = outs
    sums[...] = jnp.zeros_like(sums)

    def fn(r):
        dh = acc[r, :] + recv[r, :].astype(f32)
        n, back = norm_back(dh, mid[r, :], vec[base + 6 : base + 7, :])
        dm = g_in[r, :].astype(f32) + back
        dm_ref[r, :] = dm
        db = (dm * vec[base + 5 : base + 6, :]).astype(bf16)
        db_ref[r, :] = db
        sums[0:1, :] += col_sum(dh * n)
        sums[1:2, :] += col_sum(dh)
        sums[2:3, :] += col_sum(dm * branch[r, :].astype(f32))
        sums[3:4, :] += col_sum(db.astype(f32))

    row_loop(acc.shape[0], fn)


def epi_dh1(acc, extra, outs, *, base, prev):
    if prev is None:
        recv, res, dm, vec = extra
        g_ref, sums = outs
    else:
        recv, res, dm, vec, down = extra
        g_ref, dd_ref, sums, dsums = outs
        dsums[...] = jnp.zeros_like(dsums)
    sums[...] = jnp.zeros_like(sums)

    def fn(r):
        dh = acc[r, :] + recv[r, :].astype(f32)
        n, back = norm_back(dh, res[r, :].astype(f32), vec[base : base + 1, :])
        g = dm[r, :] + back
        g_ref[r, :] = g
        sums[0:1, :] += col_sum(dh * n)
        sums[1:2, :] += col_sum(dh)
        if prev is not None:
            dd = (g * vec[prev + 9 : prev + 10, :]).astype(bf16)
            dd_ref[r, :] = dd
            dsums[0:1, :] += col_sum(g * down[r, :].astype(f32))
            dsums[1:2, :] += col_sum(dd.astype(f32))

    row_loop(acc.shape[0], fn)


def dw_kernel(ids, a_t, b, *rest, n_add, n_old, flat):
    y = dot(a_t[...], b[...].reshape(b.shape[-2:]))
    if n_add:
        y = y + rest[0][...].astype(f32)
    rest = rest[n_add + n_old :]
    if flat:
        rest[0][...] = y.astype(bf16)
        return
    keep, send, acc = rest
    acc[...] = y
    rows = keep.shape[1]
    for q in range(4):
        for bit, out in ((ids[IY], keep), (1 - ids[IY], send)):
            at = pl.multiple_of((2 * q + bit) * rows, rows)
            out[q] = acc[pl.ds(at, rows), :].astype(bf16)


def dw_call(ids, a_t, b, bspec, n, adds, name, flat=False, total=None, col=0, old=()):
    wide, tokens = a_t.shape
    nb = 256

    def cols(at):
        return pl.BlockSpec((wide, nb), lambda j, ids: (0, at // nb + j))

    if flat:
        outs = [((wide, total), bf16, cols(col))]
        scratch = []
    else:
        ospec = pl.BlockSpec((4, wide // 8, nb), lambda j, ids: (0, 0, col // nb + j))
        outs = [((4, wide // 8, total), bf16, ospec)] * 2
        scratch = [pltpu.VMEM((wide, nb), f32)]
    ins = [(a_t, whole(a_t)), (b, bspec)] + [(a, cols(at)) for a, at in adds]
    n_in = 1 + len(ins)
    ins += [(a, pl.BlockSpec(memory_space=pl.ANY)) for a in old]
    return call(
        functools.partial(dw_kernel, n_add=len(adds), n_old=len(old), flat=flat),
        (n // nb,),
        ins,
        outs,
        scratch,
        ids=ids,
        aliases={n_in + i: i for i in range(len(old))},
        name=name,
    )


def chunks_of(length):
    return [(s, min(256, length - s)) for s in range(0, length, 256)]


def head_lanes(rows, h):
    lane = lax.broadcasted_iota(jnp.int32, (rows, 2 * HD), 1)
    return (lane // HD) == h, lane == (1 - h) * HD


def attn_fwd_kernel(q_ref, k_ref, v_ref, mb_ref, o_ref, wide_ref, lse_ref):
    h = pl.program_id(0) % 2
    length = q_ref.shape[0]
    mine, mark = head_lanes(length, h)
    k0 = jnp.where(mine, k_ref[...].astype(f32), jnp.where(mark, mb_ref[...], 0.0)).astype(bf16)
    v_t = jnp.where(mine, v_ref[...].astype(f32), 1.0).astype(bf16).T
    for start, size in chunks_of(length):
        rows = pl.ds(start, size)
        mine_c, mark_c = head_lanes(size, h)
        q0 = jnp.where(mine_c, q_ref[rows, :].astype(f32), jnp.where(mark_c, 1.0, 0.0)).astype(bf16)
        s = dot(k0, q0, NT)
        top = jnp.max(s, axis=0, keepdims=True)
        p = jnp.exp(s - top).astype(bf16)
        o_t = dot(v_t, p)
        total = jnp.where(h == 0, o_t[HD : HD + 1, :], o_t[0:1, :])
        o = (o_t * (1.0 / total)).T
        o = jnp.where(mine_c, o, wide_ref[rows, :])
        wide_ref[rows, :] = o
        o_ref[rows, :] = o.astype(bf16)
        lse_ref[0, :, rows] = top + jnp.log(total)


def attn_fwd(qkv, mb):
    length, wide = qkv.shape
    pairs = wide // 3 // (2 * HD)
    blk = lambda off: pl.BlockSpec((length, 2 * HD), lambda g: (0, off + g // 2))
    return call(
        attn_fwd_kernel,
        (2 * pairs,),
        [(qkv, blk(0)), (qkv, blk(pairs)), (qkv, blk(2 * pairs)), (mb, whole(mb))],
        [
            ((length, wide // 3), bf16, blk(0)),
            ((length, wide // 3), f32, blk(0)),
            ((2 * pairs, 1, length), f32, pl.BlockSpec((1, 1, length), lambda g: (g, 0, 0))),
        ],
        us=30,
        name="attn_fwd",
    )


def attn_bwd_kernel(q_ref, k_ref, v_ref, do_ref, o_ref, mb_ref, lse_ref, g_ref, sums, dk_acc, dv_acc):
    h = pl.program_id(0) % 2
    length = q_ref.shape[0]
    mine, mark = head_lanes(length, h)
    kf = k_ref[...].astype(f32)
    k0 = jnp.where(mine, kf, jnp.where(mark, mb_ref[...], 0.0)).astype(bf16)
    k_t = k_ref[...].T
    v0 = jnp.where(mine, v_ref[...].astype(f32), 0.0).astype(bf16)
    for ci, (start, size) in enumerate(chunks_of(length)):
        rows = pl.ds(start, size)
        mine_c, mark_c = head_lanes(size, h)
        q = q_ref[rows, :]
        q0 = jnp.where(mine_c, q.astype(f32), jnp.where(mark_c, 1.0, 0.0)).astype(bf16)
        do = do_ref[rows, :]
        inner = jnp.where(mine_c, do.astype(f32) * o_ref[rows, :], 0.0)
        delta = jnp.sum(inner.T, axis=0, keepdims=True)
        p = jnp.exp(dot(k0, q0, NT) - lse_ref[0, :, rows])
        ds = (p * (dot(v0, do, NT) - delta)).astype(bf16)
        dv = dot(p.astype(bf16), do)
        dk = dot(ds, q)
        if ci == 0:
            dv_acc[...] = dv
            dk_acc[...] = dk
        else:
            dv_acc[...] += dv
            dk_acc[...] += dk
        dq = dot(k_t, ds).T * HD ** (-0.5)
        g_ref[0, rows, :] = jnp.where(mine_c, dq, g_ref[0, rows, :].astype(f32)).astype(bf16)
    g_ref[1] = jnp.where(mine, dk_acc[...], g_ref[1].astype(f32)).astype(bf16)
    g_ref[2] = jnp.where(mine, dv_acc[...], g_ref[2].astype(f32)).astype(bf16)

    @pl.when(h == 1)
    def _():
        sums[0] = col_sum(g_ref[0].astype(f32))
        sums[1] = col_sum(g_ref[2].astype(f32))


def attn_bwd(qkv, d_mixed, mixed, mb, lse):
    length, wide = qkv.shape
    pairs = wide // 3 // (2 * HD)
    blk = lambda off: pl.BlockSpec((length, 2 * HD), lambda g: (0, off + g // 2))
    return call(
        attn_bwd_kernel,
        (2 * pairs,),
        [
            (qkv, blk(0)),
            (qkv, blk(pairs)),
            (qkv, blk(2 * pairs)),
            (d_mixed, blk(0)),
            (mixed, blk(0)),
            (mb, whole(mb)),
            (lse, pl.BlockSpec((1, 1, length), lambda g: (g, 0, 0))),
        ],
        [
            (
                (3, length, wide // 3),
                bf16,
                pl.BlockSpec((3, length, 2 * HD), lambda g: (0, 0, g // 2)),
            ),
            ((2, 1, wide // 3), f32, pl.BlockSpec((2, 1, 2 * HD), lambda g: (0, 0, g // 2))),
        ],
        [pltpu.VMEM((length, 2 * HD), f32), pltpu.VMEM((length, 2 * HD), f32)],
        us=30,
        name="attn_bwd",
    )


def ln_kernel(x, vec, out, *, base):
    def fn(r):
        center, rstd = norm_stats(x[r, :].astype(f32))
        out[r, :] = (center * rstd * vec[base : base + 1, :] + vec[base + 1 : base + 2, :]).astype(bf16)

    row_loop(x.shape[0], fn)


def ln_call(x, vec, base):
    return call(
        functools.partial(ln_kernel, base=base),
        (1,),
        [(x, whole(x)), (vec, whole(vec))],
        [(x.shape, bf16, whole(x))],
        name="ln",
    )[0]


def vec_grad_kernel(ids, ln1, qv, ln2, down, ub_o, ub_t, out):
    out[...] = jnp.zeros_like(out)
    n = qv.shape[2]
    at = pl.multiple_of(ids[IC] * n, n)
    out[0:2, :] = ln1[0:2, :]
    out[2:3, pl.ds(at, n)] = qv[0]
    out[3:4, pl.ds(at, n)] = qv[1]
    out[4:5, :] = ln2[3:4, :]
    out[5:6, :] = ln2[2:3, :]
    out[6:8, :] = ln2[0:2, :]
    out[8:9, :] = down[1:2, :]
    out[9:10, :] = down[0:1, :]
    row = 10 + 2 * ids[IC]
    out[pl.ds(row + ids[IX], 1), :] = ub_o[...]
    out[pl.ds(row + 1 - ids[IX], 1), :] = ub_t[...]


def adam_math(w, g, m, v, rate, decay):
    m1 = B1 * m + (1.0 - B1) * g
    v1 = B2 * v + (1.0 - B2) * g * g
    step = -rate * (
        (m1 * (1.0 / (1.0 - B1**STEPS))) / (jnp.sqrt(v1 * (1.0 / (1.0 - B2**STEPS))) + ADAM_EPS)
        + decay * w.astype(f32)
    )
    return step, m1, v1


def adam_kernel(ids, *rest, pick, n_g, n_old):
    gs = rest[:n_g]
    w, m, v = rest[n_g : n_g + 3]
    g_out, s_out, m_out, v_out = rest[n_g + 3 + n_old :]
    g = pick(ids, pl.program_id(0), gs)
    step, m1, v1 = adam_math(w[0], g, m[0], v[0], RATE_M, DECAY)
    g_out[0] = g
    s_out[0] = step
    m_out[0] = m1
    v_out[0] = v1


def pick_attn(ids, b, gs):
    own, oth = [g[...].astype(f32) for g in gs]
    return jnp.where((b % 2) == ids[IC], own, oth)


def pick_mlp(ids, b, gs):
    own, oth = gs
    core = ((b // 2) % 2) == ids[IC]
    at = pl.ds(((b % 2) + ids[IX]) % 2, 1)
    return jnp.where(core, own[at][0].astype(f32), oth[at][0].astype(f32))


def adam_call(ids, layer, gs, gspecs, w, m, v, nb, pick, old, name):
    spec = pl.BlockSpec((1, w.shape[1], nb), lambda b, ids: (layer, 0, b))
    ins = list(zip(gs, gspecs)) + [(w, spec), (m, spec), (v, spec)]
    n_in = len(ins) + 1
    ins += [(o, pl.BlockSpec(memory_space=pl.ANY)) for o in old]
    return call(
        functools.partial(adam_kernel, pick=pick, n_g=len(gs), n_old=len(old)),
        (w.shape[2] // nb,),
        ins,
        [(w.shape, f32, spec)] * 4,
        ids=ids,
        aliases={n_in + i: i for i in range(len(old))},
        name=name,
    )


def copy_kernel(ids, a, out):
    out[...] = a[0]


def pick_columns(ids, a, layer, nb, steps, index, name):
    rows = a.shape[1]
    return call(
        copy_kernel,
        (steps,),
        [(a, pl.BlockSpec((1, rows, nb), lambda j, ids: (layer, 0, index(j, ids))))],
        [((rows, nb * steps), bf16, pl.BlockSpec((rows, nb), lambda j, ids: (0, j)))],
        ids=ids,
        name=name,
    )[0]


SWAP = [(0, 1), (1, 0)]


def swap_core(a):
    return lax.ppermute(a, "seq", SWAP)


def swap_x(a):
    return lax.ppermute(a, "dp", SWAP)


def swap_bit(a, bit):
    return lax.ppermute(a, "fsdp", [(i, i ^ bit) for i in range(8)])


def merge_kernel(ids, own, recv, out, *, bit):
    mine = pl.program_id(1) == ids[bit]

    @pl.when(mine)
    def _():
        out[0] = own[...]

    @pl.when(jnp.logical_not(mine))
    def _():
        out[0] = recv[...]


def merge(ids, own, recv, bit):
    a, b, n = own.shape
    ins = pl.BlockSpec((1, b, n), lambda i, j, ids: (i, 0, 0))
    (out,) = call(
        functools.partial(merge_kernel, bit=bit),
        (a, 2),
        [(own, ins), (recv, ins)],
        [((a, 2, b, n), own.dtype, pl.BlockSpec((1, 1, b, n), lambda i, j, ids: (i, j, 0, 0)))],
        ids=ids,
        name="merge",
    )
    return out.reshape(2 * a, b, n)


def merge_z_kernel(ids, *rest):
    out = rest[-1]
    z = 2 * ids[IZ1] + ids[IZ0]
    for k, part in enumerate(rest[:-1]):
        out[pl.ds((z - k + 4) % 4, 1)] = part[...][None]


def gather_z(ids, own):
    parts = [own] + [
        lax.ppermute(own, "fsdp", [(i, (i + 2 * k) % 8) for i in range(8)]) for k in range(1, 4)
    ]
    b, n = own.shape
    nb = 512
    ins = pl.BlockSpec((b, nb), lambda j, ids: (0, j))
    return call(
        merge_z_kernel,
        (n // nb,),
        [(p, ins) for p in parts],
        [((4, b, n), own.dtype, pl.BlockSpec((4, b, nb), lambda j, ids: (0, 0, j)))],
        ids=ids,
        name="merge_z",
    )[0]


def fold_kernel(ids, keep, recv, keep_out, send_out, *, bit):
    for a in range(keep_out.shape[0]):
        for b, out in ((ids[bit], keep_out), (1 - ids[bit], send_out)):
            at = 2 * a + b
            v = keep[pl.ds(at, 1)].astype(f32) + recv[pl.ds(at, 1)].astype(f32)
            out[a] = v[0].astype(bf16)


def fold(ids, keep, recv, bit):
    a, b, n = keep.shape
    nb = 512
    ins = pl.BlockSpec((a, b, nb), lambda j, ids: (0, 0, j))
    outs = pl.BlockSpec((a // 2, b, nb), lambda j, ids: (0, 0, j))
    return call(
        functools.partial(fold_kernel, bit=bit),
        (n // nb,),
        [(keep, ins), (recv, ins)],
        [((a // 2, b, n), bf16, outs)] * 2,
        ids=ids,
        name="fold",
    )


def apart(go, fn, *args):
    def empty(*args):
        return jax.tree.map(lambda v: jnp.zeros(v.shape, v.dtype), jax.eval_shape(fn, *args))

    return lax.cond(go, fn, empty, *args)


def tie(*arrays):
    return lax.optimization_barrier(arrays)


def local(
    tokens_in,
    key_mask,
    attn_weights,
    mlp_weights,
    vectors,
    cotangent,
    first_attn,
    second_attn,
    first_mlp,
    second_mlp,
    first_vec,
    second_vec,
):
    layers, shard, _ = attn_weights.shape
    n_fsdp = lax.axis_size("fsdp")
    staged = n_fsdp == 8
    c = lax.axis_index("seq")
    x = lax.axis_index("dp")
    f = lax.axis_index("fsdp")
    ids = jnp.stack([f // 4 % 2, f // 2 % 2, f % 2, c, x]).astype(jnp.int32)

    tokens = tokens_in[0]
    go = key_mask[0, 0] >= 0
    cot = cotangent[0]
    half, wide = tokens.shape
    length = 2 * half
    group = wide // 2
    bias = jnp.where(key_mask[0] > 0, 0.0, -1e30).astype(f32).reshape(2, half)
    bias = jnp.where(c == 0, bias, bias[::-1]).reshape(length, 1)
    mb = jnp.broadcast_to(bias, (length, 2 * HD))

    pa = [
        pick_columns(ids, attn_weights, l, group, 4, lambda j, ids: 2 * j + ids[IC], "pick_a")
        for l in range(layers)
    ]
    pm = [
        pick_columns(
            ids, mlp_weights, l, wide, 2, lambda j, ids: 4 * j + 2 * ids[IC] + ids[IX], "pick_m"
        )
        for l in range(layers)
    ]
    pv = vectors.reshape(1, layers * ROWS, -1)
    def line(p, bits):
        for bit, at in bits:
            p = merge(ids, p, swap_bit(p, bit), at)
        return p

    Z1, Z0, Y = (4, IZ1), (2, IZ0), (1, IY)
    if staged:
        vec = line(pv, (Z1, Z0, Y))
    else:
        vec = lax.all_gather(pv, "fsdp", axis=0, tiled=True)
    vec = vec.transpose(1, 0, 2).reshape(layers * ROWS, -1).astype(f32)

    h_own = ln_call(tokens, vec, 0)
    h_own, *pm = tie(h_own, *pm)
    h_oth = apart(go, swap_core, h_own)
    wa, wm = [None] * layers, [None] * layers
    for l in range(layers):
        a = pa[l]
        if staged and l == 1:
            a, z4 = tie(a, z4)
        wa[l] = lax.all_gather(a, "fsdp", axis=0, tiled=True)
        if not staged:
            w = lax.all_gather(pm[l], "fsdp", axis=0, tiled=True)
            wm[l] = [w, swap_x(w)]
        elif l == 0:
            z4 = gather_z(ids, pm[0])

    vspec = pl.BlockSpec(vec.shape, lambda *_: (0, 0))
    V = (vec, vspec)
    own = pl.BlockSpec((half, wide), lambda *_: (0, 0))

    def xs(row, kb):
        return pl.BlockSpec((half, kb), lambda k, ids: (row, k))

    def fixed(shape):
        return pl.BlockSpec(shape, lambda *_: (0,) * len(shape))

    KB = 512
    nb = 256
    colspec = pl.BlockSpec((length, nb), lambda j, ids: (0, j))
    send_out = [((half, wide), bf16, own)]
    res = tokens
    saved = []
    for l in range(layers):
        base = l * ROWS
        if staged and l == 0:
            h_oth, z4 = tie(h_oth, z4)
            y0 = swap_bit(z4, 1)
            far_a = swap_x(z4)
            pm_next, _ = tie(pm[1][None], z4)
        if staged and l == 1:
            h_oth, y1 = tie(h_oth, y1)
            z4 = m_four
        qkv, h_t = nn_call(
            ids, h_own, h_oth, wa[l], 0, 3, group, functools.partial(epi_qkv, base=base), [V],
            [((length, 3 * group), bf16, pl.BlockSpec((length, group), lambda j, ids: (0, j)))],
            "qkv", flip=True,
        )
        if staged and l == 1:
            qkv, far_a = tie(qkv, far_a)
        mixed, mixed_wide, lse = attn_fwd(qkv, mb)
        if staged and l == 0:
            m_recv = swap_bit(pm_next, 4)
            mixed, y0, far_a, m_recv = tie(mixed, y0, far_a, m_recv)
            wm[0] = [(z4, y0), (far_a, swap_x(y0))]
            m_two = merge(ids, pm_next, m_recv, IZ1)
            m_recv = swap_bit(m_two, 2)
        if staged and l == 1:
            far_b = swap_x(y1)
            mixed, far_b = tie(mixed, far_b)
            wm[1] = [(z4, y1), (far_a, far_b)]

        def proj_pair(mixed, w, res, vec):
            def proj(row, epi, extra, outs):
                return nt_call(
                    ids, [(mixed, xs(row, KB), w, 3 * group)], group // KB, KB, half, wide, epi,
                    extra, outs, "proj",
                )

            (part,) = proj(1, epi_send, [], send_out)
            mid, branch, h2_own = proj(
                0, functools.partial(epi_proj, base=base),
                [(swap_core(part), own), (res, own), (vec, vspec)],
                [((half, wide), f32, own), ((half, wide), bf16, own), ((half, wide), bf16, own)],
            )
            return mid, branch, h2_own, swap_core(h2_own)

        mid, branch, h2_own, h2_oth = apart(go, proj_pair, mixed, wa[l], res, vec)
        act, gp = [], []
        for i in (0, 1):
            if staged and l == 0 and i == 1:
                h2_own, m_recv = tie(h2_own, m_recv)
                m_four = merge(ids, m_two, m_recv, IZ0)
                y1 = swap_bit(m_four, 1)
                far_a = swap_x(m_four)
            got = nn_call(
                ids, h2_own, h2_oth, wm[l][i], 0, wide // nb, nb,
                functools.partial(epi_up, base=base, own=i == 0), [V],
                [((length, wide), bf16, colspec)] * 2, "up", flip=i == 0,
            )
            act.append(got[0])
            gp.append(got[1])
            if i == 0:
                h2_t = got[2]

        last = l == layers - 1

        def down_pair(act, wm, mid, vec, cot):
            def down(row, epi, extra, outs):
                return nt_call(
                    ids, [(act[i], xs(row, KB), wm[i], wide) for i in (0, 1)],
                    wide // KB, KB, half, wide, epi, extra, outs, "down",
                )

            (part,) = down(1, epi_send, [], send_out)
            recv = swap_core(part)
            if last:
                out, dd_own, dsums = down(
                    0, functools.partial(epi_down_last, base=base),
                    [(recv, own), (mid, own), (vec, vspec), (cot, own)],
                    [((half, wide), f32, own), ((half, wide), bf16, own), ((2, wide), f32, fixed((2, wide)))],
                )
                return out, dd_own, dsums, swap_core(dd_own)
            out, down_out, h_next = down(
                0, functools.partial(epi_down, base=base, nxt=base + ROWS),
                [(recv, own), (mid, own), (vec, vspec)],
                [((half, wide), f32, own), ((half, wide), bf16, own), ((half, wide), bf16, own)],
            )
            return out, h_next, down_out, swap_core(h_next)

        out, next_own, extra_out, next_oth = apart(go, down_pair, act, wm[l], mid, vec, cot)
        if last:
            dd_own, dd_oth, dsums, down_out = next_own, next_oth, extra_out, None
        else:
            down_out = extra_out
        saved.append((res, h_t, qkv, mixed, mixed_wide, lse, mid, branch, h2_t, act, gp, down_out))
        if not last:
            res, h_own, h_oth = out, next_own, next_oth
    tokens_out = out

    g = cot
    old_a, old_m = [], []
    gvecs = [None] * layers
    pend = {}

    def step_y(key, parts):
        if staged:
            pend[key] = (parts[0], swap_bit(parts[1], 1))
        else:
            pend[key] = lax.psum_scatter(parts[0], "fsdp", scatter_dimension=0, tiled=True)

    def tied(key, other):
        other, pend[key] = tie(other, pend[key])
        return other

    def step_z0(key):
        keep, send = fold(ids, *pend[key], IZ0)
        pend[key] = (keep, swap_bit(send, 2))

    def step_z1(key):
        keep, send = fold(ids, *pend[key], IZ1)
        pend[key] = (keep, swap_bit(send, 4))

    def step_end(key):
        keep, recv = pend[key]
        return keep[0].astype(f32) + recv[0].astype(f32)

    for l in reversed(range(layers)):
        base = l * ROWS
        lower = l > 0
        split = not lower
        flat = lower or not staged
        res, h_t, qkv, mixed, mixed_wide, lse, mid, branch, h2_t, act, gp, _ = saved[l]
        du, ub = [None, None], [None, None]
        for i in (1, 0):
            got = nn_call(
                ids, dd_own, dd_oth, wm[l][i], wide, wide // nb, nb, epi_dact,
                [(gp[i], colspec)],
                [((length, wide), bf16, colspec), ((1, wide), f32, pl.BlockSpec((1, nb), lambda j, ids: (0, j)))],
                "dact", flip=i == 1,
            )
            du[i], ub[i] = got[:2]
            if i == 1:
                dd_t = got[2]
                if split:
                    far = []
                    for a_t, b in ((h2_t, du[1]), (dd_t, act[1])):
                        far += dw_call(ids, a_t, b, colspec, wide, [], "dw_far", flat=True, total=wide)
                    dd_own, *_ = tie(dd_own, *far)
                    far = [swap_x(v) for v in far]
        if not split:
            d_m = ()
            for n, (a_t, b) in enumerate(((h2_t, du[0]), (dd_t, act[0]), (h2_t, du[1]), (dd_t, act[1]))):
                d_m = dw_call(
                    ids, a_t, b, colspec, wide, [], "dw_mlp", flat=True, total=4 * wide, col=n * wide, old=d_m
                )
            du[0], d_m = tie(du[0], d_m[0])
            pend[("m", l)] = lax.psum_scatter(d_m, "fsdp", scatter_dimension=0, tiled=True)

        def dh2_pair(du, wm, mid, g, branch, vec):
            def dh2(row, epi, extra, outs):
                return nt_call(
                    ids, [(du[i], xs(row, KB), wm[i], 0) for i in (0, 1)],
                    wide // KB, KB, half, wide, epi, extra, outs, "dh2",
                )

            (part,) = dh2(1, epi_send, [], send_out)
            dm, db_own, sums2 = dh2(
                0, functools.partial(epi_dh2, base=base),
                [(swap_core(part), own), (mid, own), (g, own), (branch, own), (vec, vspec)],
                [((half, wide), f32, own), ((half, wide), bf16, own), ((4, wide), f32, fixed((4, wide)))],
            )
            return dm, db_own, sums2, swap_core(db_own)

        dm, db_own, sums2, db_oth = apart(go, dh2_pair, du, wm[l], mid, g, branch, vec)
        if split:
            db_oth, pend[("m", l + 1)] = tie(db_oth, pend[("m", l + 1)])
            d_up, _ = tie(pend[("a", l + 1)], pend[("m", l + 1)])
            pend[("a", l + 1)] = lax.psum_scatter(d_up, "fsdp", scatter_dimension=0, tiled=True)
        d_mixed, db_t = nn_call(
            ids, db_own, db_oth, wa[l], 3 * group, group // nb, nb, epi_plain, [],
            [((length, group), bf16, colspec)], "dmixed", flip=True,
        )
        d_a = dw_call(
            ids, db_t, mixed, colspec, group, [], "dw_p", flat=flat, total=4 * group, col=3 * group
        )
        d_mixed, d_a = tie(d_mixed, d_a)
        d_qkv, qv = attn_bwd(qkv, d_mixed, mixed_wide, mb, lse)
        qspec = pl.BlockSpec((1, length, nb), lambda j, ids: (j * nb // group, 0, j % (group // nb)))
        d_a = dw_call(
            ids, h_t, d_qkv, qspec, 3 * group, [], "dw_qkv", flat=flat, total=4 * group, old=d_a
        )
        d_qkv, d_a = tie(d_qkv, d_a)
        if not split:
            pend[("a", l)] = d_a[0]
        else:
            step_y("a", d_a)
            d_qkv, *far = tie(d_qkv, *far)
            near = ()
            for n, (a_t, b) in enumerate(((h2_t, du[0]), (dd_t, act[0]))):
                near = dw_call(
                    ids, a_t, b, colspec, wide, [(far[n], 0)], "dw_near", flat=flat,
                    total=2 * wide, col=n * wide, old=near,
                )
            d_qkv, near = tie(d_qkv, near)
            step_y("m", near)
        down_below = saved[l - 1][-1] if lower else None

        def dh1_pair(d_qkv, w, res, dm, vec, down_below):
            def dh1(row, epi, extra, outs):
                spec = pl.BlockSpec((1, half, group), lambda k, ids: (k, row, 0))
                return nt_call(ids, [(d_qkv, spec, w, 0)], 3, group, half, wide, epi, extra, outs, "dh1")

            (part,) = dh1(1, epi_send, [], send_out)
            extra = [(swap_core(part), own), (res, own), (dm, own), (vec, vspec)]
            outs = [((half, wide), f32, own), ((2, wide), f32, fixed((2, wide)))]
            if lower:
                extra.append((down_below, own))
                outs[1:1] = [((half, wide), bf16, own)]
                outs.append(((2, wide), f32, fixed((2, wide))))
            got = dh1(0, functools.partial(epi_dh1, base=base, prev=base - ROWS if lower else None), extra, outs)
            return got, swap_core(got[1]) if lower else ()

        got, below_oth = apart(go, dh1_pair, d_qkv, wa[l], res, dm, vec, down_below)
        sums1 = got[2] if lower else got[1]

        (gvecs[l],) = call(
            vec_grad_kernel,
            (1,),
            [(a, whole(a)) for a in (sums1, qv, sums2, dsums, ub[0], ub[1])],
            [((16, wide), f32, fixed((16, wide)))],
            ids=ids,
            name="vec_grad",
        )
        g = got[0]
        if lower:
            dd_own, dd_oth, dsums = got[1], below_oth, got[3]
    grad_tokens = g

    for l in reversed(range(layers)):
        if l == 0 and staged:
            pend["a"], old_a, old_m = tie(pend["a"], tuple(old_a), tuple(old_m))
            for step in (step_z0, step_z1):
                for key in ("a", "m"):
                    step(key)
            g_a, g_m = step_end("a").astype(bf16), step_end("m").astype(bf16)
        elif l == 0:
            g_a, g_m = pend["a"], pend["m"]
        else:
            g_a, g_m = pend[("a", l)], pend[("m", l)]
        g_a = (g_a.astype(f32) + swap_x(g_a).astype(f32)).astype(bf16)
        if l > 0:
            r_m = swap_x(g_m)
            n = 2 * wide
            g_m = jnp.stack(
                [
                    (g_m[:, :n].astype(f32) + r_m[:, n:].astype(f32)).astype(bf16),
                    (g_m[:, n:].astype(f32) + r_m[:, :n].astype(f32)).astype(bf16),
                ]
            )
        else:
            g_m = jnp.stack([g_m, swap_x(g_m)])
        g_mt = swap_core(g_m)
        g_at = swap_core(g_a)
        aspec = pl.BlockSpec((shard, group), lambda b, ids: (0, b // 2))
        old_a = adam_call(
            ids, l, [g_a, g_at], [aspec, aspec], attn_weights, first_attn, second_attn,
            group, pick_attn, old_a, "adam_attn",
        )
        mspec = pl.BlockSpec((2, shard, wide), lambda b, ids: (0, 0, b // 4))
        old_m = adam_call(
            ids, l, [g_m, g_mt], [mspec] * 2, mlp_weights, first_mlp, second_mlp,
            wide, pick_mlp, old_m, "adam_mlp",
        )

    gv = jnp.stack(gvecs)
    if staged:
        gv = gv + swap_core(gv)
        gv = gv + swap_x(gv)
        for bit in (1, 2, 4):
            gv = gv + swap_bit(gv, bit)
    else:
        gv = lax.psum(gv, ("dp", "fsdp", "seq"))
    gv = lax.dynamic_slice_in_dim(gv, f * (wide // n_fsdp), wide // n_fsdp, axis=2)
    gv = gv[:, :ROWS]
    step_v, one_v, two_v = adam_math(vectors, gv, first_vec, second_vec, RATE_V, 0.0)

    return (
        tokens_out[None],
        grad_tokens[None],
        old_a[0],
        old_m[0],
        gv,
        old_a[1],
        old_m[1],
        step_v,
        old_a[2],
        old_a[3],
        old_m[2],
        old_m[3],
        one_v,
        two_v,
    )


def solution(mesh):
    tok = P(("dp", "fsdp"), "seq", None)
    mat = P(None, "fsdp", None)
    vec = P(None, None, "fsdp")
    return jax.shard_map(
        local,
        mesh=mesh,
        in_specs=(tok, P(("dp", "fsdp"), None), mat, mat, vec, tok, mat, mat, mat, mat, vec, vec),
        out_specs=(tok, tok, mat, mat, vec, mat, mat, vec, mat, mat, mat, mat, vec, vec),
        check_vma=False,
    )
```

```python
import functools

import jax
import jax.numpy as jnp
from jax import lax
from jax.experimental import pallas as pl
from jax.experimental.pallas import tpu as pltpu
from jax.sharding import PartitionSpec as P

HD = 64
EPS = 1e-06
B1 = 0.9
B2 = 0.999
ADAM_EPS = 1e-08
DECAY = 0.05
RATE_M = 0.01
RATE_V = 0.05
STEPS = 10.0
ROWS = 14
IZ1, IZ0, IY, IC, IX = range(5)

f32 = jnp.float32
bf16 = jnp.bfloat16
NN = (((1,), (0,)), ((), ()))
NT = (((1,), (1,)), ((), ()))
TN = (((0,), (0,)), ((), ()))
MB = 1 << 20


def dot(a, b, dims=NN):
    return lax.dot_general(a, b, dims, preferred_element_type=f32)


def sds(shape, dtype):
    return jax.ShapeDtypeStruct(shape, dtype)


def call(body, grid, ins, outs, scratch=(), ids=None, us=2, vmem=40, aliases=None, name=None):
    n_pre = 0 if ids is None else 1
    moved = sum(a.size * a.dtype.itemsize for a, s in ins if s.block_shape is not None)
    moved += sum(
        functools.reduce(lambda p, q: p * q, sh, 1) * jnp.dtype(dt).itemsize for sh, dt, _ in outs
    )
    return pl.pallas_call(
        body,
        out_shape=[sds(sh, dt) for sh, dt, _ in outs],
        grid_spec=pltpu.PrefetchScalarGridSpec(
            num_scalar_prefetch=n_pre,
            grid=grid,
            in_specs=[s for _, s in ins],
            out_specs=[s for _, _, s in outs],
            scratch_shapes=list(scratch),
        ),
        compiler_params=pltpu.CompilerParams(vmem_limit_bytes=vmem * MB),
        cost_estimate=pl.CostEstimate(flops=1, bytes_accessed=1, transcendentals=0),
        input_output_aliases=aliases or {},
        name=name,
    )(*(() if ids is None else (ids,)), *[a for a, _ in ins])


def whole(a):
    nd = a.ndim
    return pl.BlockSpec(a.shape, lambda *_: (0,) * nd)


def row_loop(total, fn):
    step = 104 if total % 104 == 0 else 8

    def body(i, carry):
        fn(pl.ds(pl.multiple_of(i * step, 8), step))
        return carry

    lax.fori_loop(0, total // step, body, 0)


def norm_stats(v):
    center = v - jnp.mean(v, axis=-1, keepdims=True)
    rstd = lax.rsqrt(jnp.mean(center * center, axis=-1, keepdims=True) + EPS)
    return center, rstd


def col_sum(v):
    return jnp.sum(v, axis=0, keepdims=True)


def weight_ins(w, rows, nb, index):
    if isinstance(w, tuple):
        spec = pl.BlockSpec((4, rows // 8, nb), lambda k, ids: (0, 0, index(k)))
        return [(p, spec) for p in w]
    return [(w, pl.BlockSpec((rows, nb), lambda k, ids: (0, index(k))))]


def weight_scratch(w, rows, nb):
    return [pltpu.VMEM((rows, nb), bf16)] if isinstance(w, tuple) else []


def weight_ref(ids, refs, spare):
    if len(refs) == 1:
        return refs[0]
    rows = refs[0].shape[1]
    for q in range(4):
        for bit, ref in ((ids[IY], refs[0]), (1 - ids[IY], refs[1])):
            spare[pl.ds(pl.multiple_of((2 * q + bit) * rows, rows), rows), :] = ref[q]
    return spare


def nn_kernel(ids, xo, xt, *rest, n_w, epi, n_extra, n_out, flip):
    w = rest[:n_w]
    extra = rest[n_w : n_w + n_extra]
    outs = rest[n_w + n_extra : n_w + n_extra + n_out]
    xf = rest[n_w + n_extra + n_out]
    half = xo.shape[0]

    @pl.when(pl.program_id(0) == 0)
    def _():
        xf[0:half, :] = xo[...]
        xf[half:, :] = xt[...]
        if flip:
            nb = 256
            for at in range(0, xf.shape[1], nb):
                outs[-1][at : at + nb, :] = xf[:, at : at + nb].T

    w = weight_ref(ids, w, rest[-1])
    epi(ids, dot(xf[...], w[...]), extra, outs)


def nn_call(ids, xo, xt, w, col, steps, nb, epi, extra, outs, name, flip=False, us=5):
    half, width = xo.shape
    outs = list(outs)
    if flip:
        shape = (width, 2 * half)
        outs.append((shape, bf16, pl.BlockSpec(shape, lambda j, ids: (0, 0))))
    wi = weight_ins(w, width, nb, lambda j: col // nb + j)
    body = functools.partial(
        nn_kernel, n_w=len(wi), epi=epi, n_extra=len(extra), n_out=len(outs), flip=flip
    )
    return call(
        body,
        (steps,),
        [(xo, whole(xo)), (xt, whole(xt))] + wi + extra,
        outs,
        [pltpu.VMEM((2 * half, width), bf16)] + weight_scratch(w, width, nb),
        ids=ids,
        us=us,
        name=name,
    )


def epi_qkv(ids, y, extra, outs, *, base):
    (vec,) = extra
    j = pl.program_id(0)
    nb = y.shape[1]
    at = pl.multiple_of(ids[IC] * nb, nb)
    qb = vec[base + 2 : base + 3, pl.ds(at, nb)]
    vb = vec[base + 3 : base + 4, pl.ds(at, nb)]
    bias = jnp.where(j == 0, qb, jnp.where(j == 2, vb, 0.0))
    scale = jnp.where(j == 0, HD ** (-0.5), 1.0)
    outs[0][...] = ((y + bias) * scale).astype(bf16)


def gelu_parts(t):
    a = jnp.abs(t)
    k = 1.0 / (1.0 + 0.23164189 * a)
    e = jnp.exp(-0.5 * t * t)
    poly = k * (
        0.127414796 + k * (-0.142248368 + k * (0.7107068705 + k * (-0.7265760135 + k * 0.5307027145)))
    )
    tail = poly * e
    phi = jnp.where(t < 0, tail, 1.0 - tail)
    return phi, e * 0.3989422804014327


def epi_up(ids, y, extra, outs, *, base, own):
    (vec,) = extra
    j = pl.program_id(0)
    nb = y.shape[1]
    half = ids[IX] if own else 1 - ids[IX]
    row = base + 10 + 2 * ids[IC] + half
    bias = vec[pl.ds(row, 1), pl.ds(pl.multiple_of(j * nb, nb), nb)]
    u = y + bias
    phi, dens = gelu_parts(u)
    outs[0][...] = (u * phi).astype(bf16)
    outs[1][...] = (phi + u * dens).astype(bf16)


def epi_dact(ids, y, extra, outs):
    (gp,) = extra
    du = (y * gp[...].astype(f32)).astype(bf16)
    outs[0][...] = du
    outs[1][...] = col_sum(du.astype(f32))


def epi_plain(ids, y, extra, outs):
    outs[0][...] = y.astype(bf16)


def nt_kernel(ids, *rest, n_ws, epi, n_extra, n_out):
    n_in = sum(1 + n for n in n_ws)
    extra = rest[n_in : n_in + n_extra]
    outs = rest[n_in + n_extra : n_in + n_extra + n_out]
    acc = rest[n_in + n_extra + n_out]
    spares = rest[n_in + n_extra + n_out + 1 :]
    k = pl.program_id(0)
    nb = 256
    pairs = []
    at = 0
    for gi, n in enumerate(n_ws):
        spare = spares[gi] if spares else None
        pairs.append((rest[at], weight_ref(ids, rest[at + 1 : at + 1 + n], spare)))
        at += 1 + n

    def body(i, carry):
        cols = pl.ds(pl.multiple_of(i * nb, nb), nb)
        y = None
        for x, w in pairs:
            xv = x[...]
            v = dot(xv.reshape(xv.shape[-2:]), w[cols, :], NT)
            y = v if y is None else y + v

        @pl.when(k == 0)
        def _():
            acc[:, cols] = y

        @pl.when(k > 0)
        def _():
            acc[:, cols] += y

        return carry

    lax.fori_loop(0, acc.shape[1] // nb, body, 0)

    @pl.when(k == pl.num_programs(0) - 1)
    def _():
        epi(acc, extra, outs)


def nt_call(ids, groups, steps, kb, rows, wide, epi, extra, outs, name):
    ins, n_ws, scratch = [], [], [pltpu.VMEM((rows, wide), f32)]
    for x, xs, w, col in groups:
        ins.append((x, xs))
        wi = weight_ins(w, wide, kb, lambda k, c=col // kb: c + k)
        ins += wi
        n_ws.append(len(wi))
        scratch += weight_scratch(w, wide, kb)
    body = functools.partial(
        nt_kernel, n_ws=tuple(n_ws), epi=epi, n_extra=len(extra), n_out=len(outs)
    )
    return call(body, (steps,), ins + extra, outs, scratch, ids=ids, us=6, name=name)


def epi_send(acc, extra, outs):
    row_loop(acc.shape[0], lambda r: outs[0].__setitem__((r, slice(None)), acc[r, :].astype(bf16)))


def epi_proj(acc, extra, outs, *, base):
    recv, res, vec = extra
    mid_ref, branch_ref, h_ref = outs

    def fn(r):
        branch = acc[r, :] + recv[r, :].astype(f32) + vec[base + 4 : base + 5, :]
        mid = res[r, :].astype(f32) + vec[base + 5 : base + 6, :] * branch
        mid_ref[r, :] = mid
        branch_ref[r, :] = branch.astype(bf16)
        center, rstd = norm_stats(mid)
        h_ref[r, :] = (
            center * rstd * vec[base + 6 : base + 7, :] + vec[base + 7 : base + 8, :]
        ).astype(bf16)

    row_loop(acc.shape[0], fn)


def epi_down(acc, extra, outs, *, base, nxt):
    recv, mid, vec = extra
    out_ref, down_ref, h_ref = outs

    def fn(r):
        down = acc[r, :] + recv[r, :].astype(f32) + vec[base + 8 : base + 9, :]
        down_ref[r, :] = down.astype(bf16)
        res = mid[r, :] + vec[base + 9 : base + 10, :] * down
        out_ref[r, :] = res
        center, rstd = norm_stats(res)
        h_ref[r, :] = (
            center * rstd * vec[nxt : nxt + 1, :] + vec[nxt + 1 : nxt + 2, :]
        ).astype(bf16)

    row_loop(acc.shape[0], fn)


def epi_down_last(acc, extra, outs, *, base):
    recv, mid, vec, cot = extra
    out_ref, dd_ref, sums = outs
    sums[...] = jnp.zeros_like(sums)

    def fn(r):
        down = acc[r, :] + recv[r, :].astype(f32) + vec[base + 8 : base + 9, :]
        scale = vec[base + 9 : base + 10, :]
        out_ref[r, :] = mid[r, :] + scale * down
        g = cot[r, :].astype(f32)
        dd = (g * scale).astype(bf16)
        dd_ref[r, :] = dd
        sums[0:1, :] += col_sum(g * down)
        sums[1:2, :] += col_sum(dd.astype(f32))

    row_loop(acc.shape[0], fn)


def norm_back(grad, values, gain):
    center, rstd = norm_stats(values)
    n = center * rstd
    e = grad * gain
    me = jnp.mean(e, axis=-1, keepdims=True)
    men = jnp.mean(e * n, axis=-1, keepdims=True)
    return n, rstd * (e - me - n * men)


def epi_dh2(acc, extra, outs, *, base):
    recv, mid, g_in, branch, vec = extra
    dm_ref, db_ref, sums = outs
    sums[...] = jnp.zeros_like(sums)

    def fn(r):
        dh = acc[r, :] + recv[r, :].astype(f32)
        n, back = norm_back(dh, mid[r, :], vec[base + 6 : base + 7, :])
        dm = g_in[r, :].astype(f32) + back
        dm_ref[r, :] = dm
        db = (dm * vec[base + 5 : base + 6, :]).astype(bf16)
        db_ref[r, :] = db
        sums[0:1, :] += col_sum(dh * n)
        sums[1:2, :] += col_sum(dh)
        sums[2:3, :] += col_sum(dm * branch[r, :].astype(f32))
        sums[3:4, :] += col_sum(db.astype(f32))

    row_loop(acc.shape[0], fn)


def epi_dh1(acc, extra, outs, *, base, prev):
    if prev is None:
        recv, res, dm, vec = extra
        g_ref, sums = outs
    else:
        recv, res, dm, vec, down = extra
        g_ref, dd_ref, sums, dsums = outs
        dsums[...] = jnp.zeros_like(dsums)
    sums[...] = jnp.zeros_like(sums)

    def fn(r):
        dh = acc[r, :] + recv[r, :].astype(f32)
        n, back = norm_back(dh, res[r, :].astype(f32), vec[base : base + 1, :])
        g = dm[r, :] + back
        g_ref[r, :] = g
        sums[0:1, :] += col_sum(dh * n)
        sums[1:2, :] += col_sum(dh)
        if prev is not None:
            dd = (g * vec[prev + 9 : prev + 10, :]).astype(bf16)
            dd_ref[r, :] = dd
            dsums[0:1, :] += col_sum(g * down[r, :].astype(f32))
            dsums[1:2, :] += col_sum(dd.astype(f32))

    row_loop(acc.shape[0], fn)


def dw_kernel(ids, a_t, b, *rest, n_add, n_old, flat):
    y = dot(a_t[...], b[...].reshape(b.shape[-2:]))
    if n_add:
        y = y + rest[0][...].astype(f32)
    rest = rest[n_add + n_old :]
    if flat:
        rest[0][...] = y.astype(bf16)
        return
    keep, send, acc = rest
    acc[...] = y
    rows = keep.shape[1]
    for q in range(4):
        for bit, out in ((ids[IY], keep), (1 - ids[IY], send)):
            at = pl.multiple_of((2 * q + bit) * rows, rows)
            out[q] = acc[pl.ds(at, rows), :].astype(bf16)


def dw_call(ids, a_t, b, bspec, n, adds, name, flat=False, total=None, col=0, old=()):
    wide, tokens = a_t.shape
    nb = 256

    def cols(at):
        return pl.BlockSpec((wide, nb), lambda j, ids: (0, at // nb + j))

    if flat:
        outs = [((wide, total), bf16, cols(col))]
        scratch = []
    else:
        ospec = pl.BlockSpec((4, wide // 8, nb), lambda j, ids: (0, 0, col // nb + j))
        outs = [((4, wide // 8, total), bf16, ospec)] * 2
        scratch = [pltpu.VMEM((wide, nb), f32)]
    ins = [(a_t, whole(a_t)), (b, bspec)] + [(a, cols(at)) for a, at in adds]
    n_in = 1 + len(ins)
    ins += [(a, pl.BlockSpec(memory_space=pl.ANY)) for a in old]
    return call(
        functools.partial(dw_kernel, n_add=len(adds), n_old=len(old), flat=flat),
        (n // nb,),
        ins,
        outs,
        scratch,
        ids=ids,
        aliases={n_in + i: i for i in range(len(old))},
        name=name,
    )


def chunks_of(length):
    return [(s, min(256, length - s)) for s in range(0, length, 256)]


def head_lanes(rows, h):
    lane = lax.broadcasted_iota(jnp.int32, (rows, 2 * HD), 1)
    return (lane // HD) == h, lane == (1 - h) * HD


def attn_fwd_kernel(q_ref, k_ref, v_ref, mb_ref, o_ref, wide_ref, lse_ref):
    h = pl.program_id(0) % 2
    length = q_ref.shape[0]
    mine, mark = head_lanes(length, h)
    k0 = jnp.where(mine, k_ref[...].astype(f32), jnp.where(mark, mb_ref[...], 0.0)).astype(bf16)
    v_t = jnp.where(mine, v_ref[...].astype(f32), 1.0).astype(bf16).T
    for start, size in chunks_of(length):
        rows = pl.ds(start, size)
        mine_c, mark_c = head_lanes(size, h)
        q0 = jnp.where(mine_c, q_ref[rows, :].astype(f32), jnp.where(mark_c, 1.0, 0.0)).astype(bf16)
        s = dot(k0, q0, NT)
        top = jnp.max(s, axis=0, keepdims=True)
        p = jnp.exp(s - top).astype(bf16)
        o_t = dot(v_t, p)
        total = jnp.where(h == 0, o_t[HD : HD + 1, :], o_t[0:1, :])
        o = (o_t * (1.0 / total)).T
        o = jnp.where(mine_c, o, wide_ref[rows, :])
        wide_ref[rows, :] = o
        o_ref[rows, :] = o.astype(bf16)
        lse_ref[0, :, rows] = top + jnp.log(total)


def attn_fwd(qkv, mb):
    length, wide = qkv.shape
    pairs = wide // 3 // (2 * HD)
    blk = lambda off: pl.BlockSpec((length, 2 * HD), lambda g: (0, off + g // 2))
    return call(
        attn_fwd_kernel,
        (2 * pairs,),
        [(qkv, blk(0)), (qkv, blk(pairs)), (qkv, blk(2 * pairs)), (mb, whole(mb))],
        [
            ((length, wide // 3), bf16, blk(0)),
            ((length, wide // 3), f32, blk(0)),
            ((2 * pairs, 1, length), f32, pl.BlockSpec((1, 1, length), lambda g: (g, 0, 0))),
        ],
        us=30,
        name="attn_fwd",
    )


def attn_bwd_kernel(q_ref, k_ref, v_ref, do_ref, o_ref, mb_ref, lse_ref, g_ref, sums, dk_acc, dv_acc):
    h = pl.program_id(0) % 2
    length = q_ref.shape[0]
    mine, mark = head_lanes(length, h)
    kf = k_ref[...].astype(f32)
    k0 = jnp.where(mine, kf, jnp.where(mark, mb_ref[...], 0.0)).astype(bf16)
    k_t = k_ref[...].T
    v0 = jnp.where(mine, v_ref[...].astype(f32), 0.0).astype(bf16)
    for ci, (start, size) in enumerate(chunks_of(length)):
        rows = pl.ds(start, size)
        mine_c, mark_c = head_lanes(size, h)
        q = q_ref[rows, :]
        q0 = jnp.where(mine_c, q.astype(f32), jnp.where(mark_c, 1.0, 0.0)).astype(bf16)
        do = do_ref[rows, :]
        inner = jnp.where(mine_c, do.astype(f32) * o_ref[rows, :], 0.0)
        delta = jnp.sum(inner.T, axis=0, keepdims=True)
        p = jnp.exp(dot(k0, q0, NT) - lse_ref[0, :, rows])
        ds = (p * (dot(v0, do, NT) - delta)).astype(bf16)
        dv = dot(p.astype(bf16), do)
        dk = dot(ds, q)
        if ci == 0:
            dv_acc[...] = dv
            dk_acc[...] = dk
        else:
            dv_acc[...] += dv
            dk_acc[...] += dk
        dq = dot(k_t, ds).T * HD ** (-0.5)
        g_ref[0, rows, :] = jnp.where(mine_c, dq, g_ref[0, rows, :].astype(f32)).astype(bf16)
    g_ref[1] = jnp.where(mine, dk_acc[...], g_ref[1].astype(f32)).astype(bf16)
    g_ref[2] = jnp.where(mine, dv_acc[...], g_ref[2].astype(f32)).astype(bf16)

    @pl.when(h == 1)
    def _():
        sums[0] = col_sum(g_ref[0].astype(f32))
        sums[1] = col_sum(g_ref[2].astype(f32))


def attn_bwd(qkv, d_mixed, mixed, mb, lse):
    length, wide = qkv.shape
    pairs = wide // 3 // (2 * HD)
    blk = lambda off: pl.BlockSpec((length, 2 * HD), lambda g: (0, off + g // 2))
    return call(
        attn_bwd_kernel,
        (2 * pairs,),
        [
            (qkv, blk(0)),
            (qkv, blk(pairs)),
            (qkv, blk(2 * pairs)),
            (d_mixed, blk(0)),
            (mixed, blk(0)),
            (mb, whole(mb)),
            (lse, pl.BlockSpec((1, 1, length), lambda g: (g, 0, 0))),
        ],
        [
            (
                (3, length, wide // 3),
                bf16,
                pl.BlockSpec((3, length, 2 * HD), lambda g: (0, 0, g // 2)),
            ),
            ((2, 1, wide // 3), f32, pl.BlockSpec((2, 1, 2 * HD), lambda g: (0, 0, g // 2))),
        ],
        [pltpu.VMEM((length, 2 * HD), f32), pltpu.VMEM((length, 2 * HD), f32)],
        us=30,
        name="attn_bwd",
    )


def ln_kernel(x, vec, out, *, base):
    def fn(r):
        center, rstd = norm_stats(x[r, :].astype(f32))
        out[r, :] = (center * rstd * vec[base : base + 1, :] + vec[base + 1 : base + 2, :]).astype(bf16)

    row_loop(x.shape[0], fn)


def ln_call(x, vec, base):
    return call(
        functools.partial(ln_kernel, base=base),
        (1,),
        [(x, whole(x)), (vec, whole(vec))],
        [(x.shape, bf16, whole(x))],
        name="ln",
    )[0]


def vec_grad_kernel(ids, ln1, qv, ln2, down, ub_o, ub_t, out):
    out[...] = jnp.zeros_like(out)
    n = qv.shape[2]
    at = pl.multiple_of(ids[IC] * n, n)
    out[0:2, :] = ln1[0:2, :]
    out[2:3, pl.ds(at, n)] = qv[0]
    out[3:4, pl.ds(at, n)] = qv[1]
    out[4:5, :] = ln2[3:4, :]
    out[5:6, :] = ln2[2:3, :]
    out[6:8, :] = ln2[0:2, :]
    out[8:9, :] = down[1:2, :]
    out[9:10, :] = down[0:1, :]
    row = 10 + 2 * ids[IC]
    out[pl.ds(row + ids[IX], 1), :] = ub_o[...]
    out[pl.ds(row + 1 - ids[IX], 1), :] = ub_t[...]


def adam_math(w, g, m, v, rate, decay):
    m1 = B1 * m + (1.0 - B1) * g
    v1 = B2 * v + (1.0 - B2) * g * g
    step = -rate * (
        (m1 * (1.0 / (1.0 - B1**STEPS))) / (jnp.sqrt(v1 * (1.0 / (1.0 - B2**STEPS))) + ADAM_EPS)
        + decay * w.astype(f32)
    )
    return step, m1, v1


def adam_kernel(ids, *rest, pick, n_g, n_old):
    gs = rest[:n_g]
    w, m, v = rest[n_g : n_g + 3]
    g_out, s_out, m_out, v_out = rest[n_g + 3 + n_old :]
    g = pick(ids, pl.program_id(0), gs)
    step, m1, v1 = adam_math(w[0], g, m[0], v[0], RATE_M, DECAY)
    g_out[0] = g
    s_out[0] = step
    m_out[0] = m1
    v_out[0] = v1


def pick_attn(ids, b, gs):
    own, oth = [g[...].astype(f32) for g in gs]
    return jnp.where((b % 2) == ids[IC], own, oth)


def pick_mlp(ids, b, gs):
    own, oth = gs
    core = ((b // 2) % 2) == ids[IC]
    at = pl.ds(((b % 2) + ids[IX]) % 2, 1)
    return jnp.where(core, own[at][0].astype(f32), oth[at][0].astype(f32))


def adam_call(ids, layer, gs, gspecs, w, m, v, nb, pick, old, name):
    spec = pl.BlockSpec((1, w.shape[1], nb), lambda b, ids: (layer, 0, b))
    ins = list(zip(gs, gspecs)) + [(w, spec), (m, spec), (v, spec)]
    n_in = len(ins) + 1
    ins += [(o, pl.BlockSpec(memory_space=pl.ANY)) for o in old]
    return call(
        functools.partial(adam_kernel, pick=pick, n_g=len(gs), n_old=len(old)),
        (w.shape[2] // nb,),
        ins,
        [(w.shape, f32, spec)] * 4,
        ids=ids,
        aliases={n_in + i: i for i in range(len(old))},
        name=name,
    )


def copy_kernel(ids, a, out):
    out[...] = a[0]


def pick_columns(ids, a, layer, nb, steps, index, name):
    rows = a.shape[1]
    return call(
        copy_kernel,
        (steps,),
        [(a, pl.BlockSpec((1, rows, nb), lambda j, ids: (layer, 0, index(j, ids))))],
        [((rows, nb * steps), bf16, pl.BlockSpec((rows, nb), lambda j, ids: (0, j)))],
        ids=ids,
        name=name,
    )[0]


SWAP = [(0, 1), (1, 0)]


def swap_core(a):
    return lax.ppermute(a, "seq", SWAP)


def swap_x(a):
    return lax.ppermute(a, "dp", SWAP)


def swap_bit(a, bit):
    return lax.ppermute(a, "fsdp", [(i, i ^ bit) for i in range(8)])


def merge_kernel(ids, own, recv, out, *, bit):
    mine = pl.program_id(1) == ids[bit]

    @pl.when(mine)
    def _():
        out[0] = own[...]

    @pl.when(jnp.logical_not(mine))
    def _():
        out[0] = recv[...]


def merge(ids, own, recv, bit):
    a, b, n = own.shape
    ins = pl.BlockSpec((1, b, n), lambda i, j, ids: (i, 0, 0))
    (out,) = call(
        functools.partial(merge_kernel, bit=bit),
        (a, 2),
        [(own, ins), (recv, ins)],
        [((a, 2, b, n), own.dtype, pl.BlockSpec((1, 1, b, n), lambda i, j, ids: (i, j, 0, 0)))],
        ids=ids,
        name="merge",
    )
    return out.reshape(2 * a, b, n)


def merge_z_kernel(ids, *rest):
    out = rest[-1]
    z = 2 * ids[IZ1] + ids[IZ0]
    for k, part in enumerate(rest[:-1]):
        out[pl.ds((z - k + 4) % 4, 1)] = part[...][None]


def gather_z(ids, own):
    parts = [own] + [
        lax.ppermute(own, "fsdp", [(i, (i + 2 * k) % 8) for i in range(8)]) for k in range(1, 4)
    ]
    b, n = own.shape
    nb = 512
    ins = pl.BlockSpec((b, nb), lambda j, ids: (0, j))
    return call(
        merge_z_kernel,
        (n // nb,),
        [(p, ins) for p in parts],
        [((4, b, n), own.dtype, pl.BlockSpec((4, b, nb), lambda j, ids: (0, 0, j)))],
        ids=ids,
        name="merge_z",
    )[0]


def fold_kernel(ids, keep, recv, keep_out, send_out, *, bit):
    for a in range(keep_out.shape[0]):
        for b, out in ((ids[bit], keep_out), (1 - ids[bit], send_out)):
            at = 2 * a + b
            v = keep[pl.ds(at, 1)].astype(f32) + recv[pl.ds(at, 1)].astype(f32)
            out[a] = v[0].astype(bf16)


def fold(ids, keep, recv, bit):
    a, b, n = keep.shape
    nb = 512
    ins = pl.BlockSpec((a, b, nb), lambda j, ids: (0, 0, j))
    outs = pl.BlockSpec((a // 2, b, nb), lambda j, ids: (0, 0, j))
    return call(
        functools.partial(fold_kernel, bit=bit),
        (n // nb,),
        [(keep, ins), (recv, ins)],
        [((a // 2, b, n), bf16, outs)] * 2,
        ids=ids,
        name="fold",
    )


def apart(go, fn, *args):
    def empty(*args):
        return jax.tree.map(lambda v: jnp.zeros(v.shape, v.dtype), jax.eval_shape(fn, *args))

    return lax.cond(go, fn, empty, *args)


def tie(*arrays):
    return lax.optimization_barrier(arrays)


def local(
    tokens_in,
    key_mask,
    attn_weights,
    mlp_weights,
    vectors,
    cotangent,
    first_attn,
    second_attn,
    first_mlp,
    second_mlp,
    first_vec,
    second_vec,
):
    layers, shard, _ = attn_weights.shape
    n_fsdp = lax.axis_size("fsdp")
    staged = n_fsdp == 8
    c = lax.axis_index("seq")
    x = lax.axis_index("dp")
    f = lax.axis_index("fsdp")
    ids = jnp.stack([f // 4 % 2, f // 2 % 2, f % 2, c, x]).astype(jnp.int32)

    tokens = tokens_in[0]
    go = key_mask[0, 0] >= 0
    cot = cotangent[0]
    half, wide = tokens.shape
    length = 2 * half
    group = wide // 2
    bias = jnp.where(key_mask[0] > 0, 0.0, -1e30).astype(f32).reshape(2, half)
    bias = jnp.where(c == 0, bias, bias[::-1]).reshape(length, 1)
    mb = jnp.broadcast_to(bias, (length, 2 * HD))

    pa = [
        pick_columns(ids, attn_weights, l, group, 4, lambda j, ids: 2 * j + ids[IC], "pick_a")
        for l in range(layers)
    ]
    pm = [
        pick_columns(
            ids, mlp_weights, l, wide, 2, lambda j, ids: 4 * j + 2 * ids[IC] + ids[IX], "pick_m"
        )
        for l in range(layers)
    ]
    pv = vectors.reshape(1, layers * ROWS, -1)
    def line(p, bits):
        for bit, at in bits:
            p = merge(ids, p, swap_bit(p, bit), at)
        return p

    Z1, Z0, Y = (4, IZ1), (2, IZ0), (1, IY)
    if staged:
        vec = line(pv, (Z1, Z0, Y))
    else:
        vec = lax.all_gather(pv, "fsdp", axis=0, tiled=True)
    vec = vec.transpose(1, 0, 2).reshape(layers * ROWS, -1).astype(f32)

    h_own = ln_call(tokens, vec, 0)
    h_own, *pm = tie(h_own, *pm)
    h_oth = apart(go, swap_core, h_own)
    wa, wm = [None] * layers, [None] * layers
    for l in range(layers):
        a = pa[l]
        if staged and l == 1:
            a, z4 = tie(a, z4)
        wa[l] = lax.all_gather(a, "fsdp", axis=0, tiled=True)
        if not staged:
            w = lax.all_gather(pm[l], "fsdp", axis=0, tiled=True)
            wm[l] = [w, swap_x(w)]
        elif l == 0:
            z4 = gather_z(ids, pm[0])

    vspec = pl.BlockSpec(vec.shape, lambda *_: (0, 0))
    V = (vec, vspec)
    own = pl.BlockSpec((half, wide), lambda *_: (0, 0))

    def xs(row, kb):
        return pl.BlockSpec((half, kb), lambda k, ids: (row, k))

    def fixed(shape):
        return pl.BlockSpec(shape, lambda *_: (0,) * len(shape))

    KB = 512
    nb = 256
    colspec = pl.BlockSpec((length, nb), lambda j, ids: (0, j))
    send_out = [((half, wide), bf16, own)]
    res = tokens
    saved = []
    for l in range(layers):
        base = l * ROWS
        if staged and l == 0:
            h_oth, z4 = tie(h_oth, z4)
            y0 = swap_bit(z4, 1)
            far_a = swap_x(z4)
            pm_next, _ = tie(pm[1][None], z4)
        if staged and l == 1:
            z4 = m_four
        qkv, h_t = nn_call(
            ids, h_own, h_oth, wa[l], 0, 3, group, functools.partial(epi_qkv, base=base), [V],
            [((length, 3 * group), bf16, pl.BlockSpec((length, group), lambda j, ids: (0, j)))],
            "qkv", flip=True,
        )
        if staged and l == 1:
            qkv, y1, far_a = tie(qkv, y1, far_a)
            far_b = swap_x(y1)
        mixed, mixed_wide, lse = attn_fwd(qkv, mb)
        if staged and l == 0:
            m_recv = swap_bit(pm_next, 4)
            mixed, y0, far_a, m_recv = tie(mixed, y0, far_a, m_recv)
            wm[0] = [(z4, y0), (far_a, swap_x(y0))]
            m_two = merge(ids, pm_next, m_recv, IZ1)
            m_recv = swap_bit(m_two, 2)
        if staged and l == 1:
            wm[1] = [(z4, y1), (far_a, far_b)]

        def proj_pair(mixed, w, res, vec):
            def proj(row, epi, extra, outs):
                return nt_call(
                    ids, [(mixed, xs(row, KB), w, 3 * group)], group // KB, KB, half, wide, epi,
                    extra, outs, "proj",
                )

            (part,) = proj(1, epi_send, [], send_out)
            mid, branch, h2_own = proj(
                0, functools.partial(epi_proj, base=base),
                [(swap_core(part), own), (res, own), (vec, vspec)],
                [((half, wide), f32, own), ((half, wide), bf16, own), ((half, wide), bf16, own)],
            )
            return mid, branch, h2_own, swap_core(h2_own)

        mid, branch, h2_own, h2_oth = apart(go, proj_pair, mixed, wa[l], res, vec)
        act, gp = [], []
        for i in (0, 1):
            if i == 1:
                h2_own, act[0] = tie(h2_own, act[0])
            got = nn_call(
                ids, h2_own, h2_oth, wm[l][i], 0, wide // nb, nb,
                functools.partial(epi_up, base=base, own=i == 0), [V],
                [((length, wide), bf16, colspec)] * 2, "up", flip=i == 0,
            )
            act.append(got[0])
            gp.append(got[1])
            if i == 0:
                h2_t = got[2]

        if staged and l == 0:
            act[0], act[1], m_recv = tie(act[0], act[1], m_recv)
            m_four = merge(ids, m_two, m_recv, IZ0)
            y1 = swap_bit(m_four, 1)
            far_a = swap_x(m_four)
        last = l == layers - 1

        def down_pair(act, wm, mid, vec, cot):
            def down(row, epi, extra, outs):
                return nt_call(
                    ids, [(act[i], xs(row, KB), wm[i], wide) for i in (0, 1)],
                    wide // KB, KB, half, wide, epi, extra, outs, "down",
                )

            (part,) = down(1, epi_send, [], send_out)
            recv = swap_core(part)
            if last:
                out, dd_own, dsums = down(
                    0, functools.partial(epi_down_last, base=base),
                    [(recv, own), (mid, own), (vec, vspec), (cot, own)],
                    [((half, wide), f32, own), ((half, wide), bf16, own), ((2, wide), f32, fixed((2, wide)))],
                )
                return out, dd_own, dsums, swap_core(dd_own)
            out, down_out, h_next = down(
                0, functools.partial(epi_down, base=base, nxt=base + ROWS),
                [(recv, own), (mid, own), (vec, vspec)],
                [((half, wide), f32, own), ((half, wide), bf16, own), ((half, wide), bf16, own)],
            )
            return out, h_next, down_out, swap_core(h_next)

        out, next_own, extra_out, next_oth = apart(go, down_pair, act, wm[l], mid, vec, cot)
        if last:
            dd_own, dd_oth, dsums, down_out = next_own, next_oth, extra_out, None
        else:
            down_out = extra_out
        saved.append((res, h_t, qkv, mixed, mixed_wide, lse, mid, branch, h2_t, act, gp, down_out))
        if not last:
            res, h_own, h_oth = out, next_own, next_oth
    tokens_out = out

    g = cot
    old_a, old_m = [], []
    gvecs = [None] * layers
    pend = {}

    def step_y(key, parts):
        if staged:
            pend[key] = (parts[0], swap_bit(parts[1], 1))
        else:
            pend[key] = lax.psum_scatter(parts[0], "fsdp", scatter_dimension=0, tiled=True)

    def tied(key, other):
        other, pend[key] = tie(other, pend[key])
        return other

    def step_z0(key):
        keep, send = fold(ids, *pend[key], IZ0)
        pend[key] = (keep, swap_bit(send, 2))

    def step_z1(key):
        keep, send = fold(ids, *pend[key], IZ1)
        pend[key] = (keep, swap_bit(send, 4))

    def step_end(key):
        keep, recv = pend[key]
        return keep[0].astype(f32) + recv[0].astype(f32)

    for l in reversed(range(layers)):
        base = l * ROWS
        lower = l > 0
        split = not lower
        flat = lower or not staged
        res, h_t, qkv, mixed, mixed_wide, lse, mid, branch, h2_t, act, gp, _ = saved[l]
        du, ub = [None, None], [None, None]
        for i in (1, 0):
            got = nn_call(
                ids, dd_own, dd_oth, wm[l][i], wide, wide // nb, nb, epi_dact,
                [(gp[i], colspec)],
                [((length, wide), bf16, colspec), ((1, wide), f32, pl.BlockSpec((1, nb), lambda j, ids: (0, j)))],
                "dact", flip=i == 1,
            )
            du[i], ub[i] = got[:2]
            if i == 1:
                dd_t = got[2]
                if split:
                    far = []
                    for a_t, b in ((h2_t, du[1]), (dd_t, act[1])):
                        far += dw_call(ids, a_t, b, colspec, wide, [], "dw_far", flat=True, total=wide)
                    dd_own, *_ = tie(dd_own, *far)
                    far = [swap_x(v) for v in far]
        if not split:
            d_m = ()
            for n, (a_t, b) in enumerate(((h2_t, du[0]), (dd_t, act[0]), (h2_t, du[1]), (dd_t, act[1]))):
                d_m = dw_call(
                    ids, a_t, b, colspec, wide, [], "dw_mlp", flat=True, total=4 * wide, col=n * wide, old=d_m
                )
            du[0], d_m = tie(du[0], d_m[0])
            pend[("m", l)] = lax.psum_scatter(d_m, "fsdp", scatter_dimension=0, tiled=True)

        def dh2_pair(du, wm, mid, g, branch, vec):
            def dh2(row, epi, extra, outs):
                return nt_call(
                    ids, [(du[i], xs(row, KB), wm[i], 0) for i in (0, 1)],
                    wide // KB, KB, half, wide, epi, extra, outs, "dh2",
                )

            (part,) = dh2(1, epi_send, [], send_out)
            dm, db_own, sums2 = dh2(
                0, functools.partial(epi_dh2, base=base),
                [(swap_core(part), own), (mid, own), (g, own), (branch, own), (vec, vspec)],
                [((half, wide), f32, own), ((half, wide), bf16, own), ((4, wide), f32, fixed((4, wide)))],
            )
            return dm, db_own, sums2, swap_core(db_own)

        dm, db_own, sums2, db_oth = apart(go, dh2_pair, du, wm[l], mid, g, branch, vec)
        if split:
            db_oth, pend[("m", l + 1)] = tie(db_oth, pend[("m", l + 1)])
            d_up, _ = tie(pend[("a", l + 1)], pend[("m", l + 1)])
            pend[("a", l + 1)] = lax.psum_scatter(d_up, "fsdp", scatter_dimension=0, tiled=True)
        d_mixed, db_t = nn_call(
            ids, db_own, db_oth, wa[l], 3 * group, group // nb, nb, epi_plain, [],
            [((length, group), bf16, colspec)], "dmixed", flip=True,
        )
        d_a = dw_call(
            ids, db_t, mixed, colspec, group, [], "dw_p", flat=flat, total=4 * group, col=3 * group
        )
        d_mixed, d_a = tie(d_mixed, d_a)
        d_qkv, qv = attn_bwd(qkv, d_mixed, mixed_wide, mb, lse)
        qspec = pl.BlockSpec((1, length, nb), lambda j, ids: (j * nb // group, 0, j % (group // nb)))
        d_a = dw_call(
            ids, h_t, d_qkv, qspec, 3 * group, [], "dw_qkv", flat=flat, total=4 * group, old=d_a
        )
        d_qkv, d_a = tie(d_qkv, d_a)
        if not split:
            pend[("a", l)] = d_a[0]
        else:
            step_y("a", d_a)
        down_below = saved[l - 1][-1] if lower else None

        def dh1_pair(d_qkv, w, res, dm, vec, down_below):
            def dh1(row, epi, extra, outs):
                spec = pl.BlockSpec((1, half, group), lambda k, ids: (k, row, 0))
                return nt_call(ids, [(d_qkv, spec, w, 0)], 3, group, half, wide, epi, extra, outs, "dh1")

            (part,) = dh1(1, epi_send, [], send_out)
            extra = [(swap_core(part), own), (res, own), (dm, own), (vec, vspec)]
            outs = [((half, wide), f32, own), ((2, wide), f32, fixed((2, wide)))]
            if lower:
                extra.append((down_below, own))
                outs[1:1] = [((half, wide), bf16, own)]
                outs.append(((2, wide), f32, fixed((2, wide))))
            got = dh1(0, functools.partial(epi_dh1, base=base, prev=base - ROWS if lower else None), extra, outs)
            return got, swap_core(got[1]) if lower else ()

        got, below_oth = apart(go, dh1_pair, d_qkv, wa[l], res, dm, vec, down_below)
        if split:
            g_first, *far = tie(got[0], *far)
            near = ()
            for n, (a_t, b) in enumerate(((h2_t, du[0]), (dd_t, act[0]))):
                near = dw_call(
                    ids, a_t, b, colspec, wide, [(far[n], 0)], "dw_near", flat=flat,
                    total=2 * wide, col=n * wide, old=near,
                )
            g_first, near = tie(g_first, near)
            step_y("m", near)
            if staged:
                pend["a"], _ = tie(pend["a"], near)
                step_z0("a")
            got = [g_first] + list(got[1:])
        sums1 = got[2] if lower else got[1]

        (gvecs[l],) = call(
            vec_grad_kernel,
            (1,),
            [(a, whole(a)) for a in (sums1, qv, sums2, dsums, ub[0], ub[1])],
            [((16, wide), f32, fixed((16, wide)))],
            ids=ids,
            name="vec_grad",
        )
        g = got[0]
        if lower:
            dd_own, dd_oth, dsums = got[1], below_oth, got[3]
    grad_tokens = g

    gv = jnp.stack(gvecs)
    if staged:
        gv, _ = tie(gv, pend["a"])
        gv = gv + swap_core(gv)
        gv = gv + swap_x(gv)
        for bit in (1, 2, 4):
            gv = gv + swap_bit(gv, bit)
    else:
        gv = lax.psum(gv, ("dp", "fsdp", "seq"))

    for l in reversed(range(layers)):
        if l == 0 and staged:
            pend["m"], pend["a"], old_a, old_m = tie(
                pend["m"], pend["a"], tuple(old_a), tuple(old_m)
            )
            step_z0("m")
            pend["m"], gv = tie(pend["m"], gv)
            step_z1("m")
            g_a, g_m = step_end("a").astype(bf16), step_end("m").astype(bf16)
        elif l == 0:
            g_a, g_m = pend["a"], pend["m"]
        else:
            g_a, g_m = pend[("a", l)], pend[("m", l)]
        g_a = (g_a.astype(f32) + swap_x(g_a).astype(f32)).astype(bf16)
        if l > 0:
            late, _ = tie(g_m, far[1])
            r_m = swap_x(late)
            if staged:
                r_m, pend["a"] = tie(r_m, pend["a"])
                step_z1("a")
            n = 2 * wide
            g_m = jnp.stack(
                [
                    (g_m[:, :n].astype(f32) + r_m[:, n:].astype(f32)).astype(bf16),
                    (g_m[:, n:].astype(f32) + r_m[:, :n].astype(f32)).astype(bf16),
                ]
            )
        else:
            g_m = jnp.stack([g_m, swap_x(g_m)])
        if l == 0:
            g_a_both = tie(g_a, swap_core(g_a))
        g_mt = swap_core(g_m)
        if l == 0:
            g_a, g_at = g_a_both
        else:
            g_at = swap_core(g_a)
        aspec = pl.BlockSpec((shard, group), lambda b, ids: (0, b // 2))
        old_a = adam_call(
            ids, l, [g_a, g_at], [aspec, aspec], attn_weights, first_attn, second_attn,
            group, pick_attn, old_a, "adam_attn",
        )
        if l == 0:
            g_m, g_mt, old_a = tie(g_m, g_mt, tuple(old_a))
        mspec = pl.BlockSpec((2, shard, wide), lambda b, ids: (0, 0, b // 4))
        old_m = adam_call(
            ids, l, [g_m, g_mt], [mspec] * 2, mlp_weights, first_mlp, second_mlp,
            wide, pick_mlp, old_m, "adam_mlp",
        )

    gv = lax.dynamic_slice_in_dim(gv, f * (wide // n_fsdp), wide // n_fsdp, axis=2)
    gv = gv[:, :ROWS]
    step_v, one_v, two_v = adam_math(vectors, gv, first_vec, second_vec, RATE_V, 0.0)

    return (
        tokens_out[None],
        grad_tokens[None],
        old_a[0],
        old_m[0],
        gv,
        old_a[1],
        old_m[1],
        step_v,
        old_a[2],
        old_a[3],
        old_m[2],
        old_m[3],
        one_v,
        two_v,
    )


def solution(mesh):
    tok = P(("dp", "fsdp"), "seq", None)
    mat = P(None, "fsdp", None)
    vec = P(None, None, "fsdp")
    return jax.shard_map(
        local,
        mesh=mesh,
        in_specs=(tok, P(("dp", "fsdp"), None), mat, mat, vec, tok, mat, mat, mat, mat, vec, vec),
        out_specs=(tok, tok, mat, mat, vec, mat, mat, vec, mat, mat, mat, mat, vec, vec),
        check_vma=False,
    )
```

```python
import functools

import jax
import jax.numpy as jnp
from jax import lax
from jax.experimental import pallas as pl
from jax.experimental.pallas import tpu as pltpu
from jax.sharding import PartitionSpec as P

HD = 64
EPS = 1e-06
B1 = 0.9
B2 = 0.999
ADAM_EPS = 1e-08
DECAY = 0.05
RATE_M = 0.01
RATE_V = 0.05
STEPS = 10.0
ROWS = 14
IZ1, IZ0, IY, IC, IX = range(5)

f32 = jnp.float32
bf16 = jnp.bfloat16
NN = (((1,), (0,)), ((), ()))
NT = (((1,), (1,)), ((), ()))
TN = (((0,), (0,)), ((), ()))
MB = 1 << 20


def dot(a, b, dims=NN):
    return lax.dot_general(a, b, dims, preferred_element_type=f32)


def sds(shape, dtype):
    return jax.ShapeDtypeStruct(shape, dtype)


def call(body, grid, ins, outs, scratch=(), ids=None, us=2, vmem=40, aliases=None, name=None):
    n_pre = 0 if ids is None else 1
    moved = sum(a.size * a.dtype.itemsize for a, s in ins if s.block_shape is not None)
    moved += sum(
        functools.reduce(lambda p, q: p * q, sh, 1) * jnp.dtype(dt).itemsize for sh, dt, _ in outs
    )
    return pl.pallas_call(
        body,
        out_shape=[sds(sh, dt) for sh, dt, _ in outs],
        grid_spec=pltpu.PrefetchScalarGridSpec(
            num_scalar_prefetch=n_pre,
            grid=grid,
            in_specs=[s for _, s in ins],
            out_specs=[s for _, _, s in outs],
            scratch_shapes=list(scratch),
        ),
        compiler_params=pltpu.CompilerParams(vmem_limit_bytes=vmem * MB),
        cost_estimate=pl.CostEstimate(flops=1, bytes_accessed=1, transcendentals=0),
        input_output_aliases=aliases or {},
        name=name,
    )(*(() if ids is None else (ids,)), *[a for a, _ in ins])


def whole(a):
    nd = a.ndim
    return pl.BlockSpec(a.shape, lambda *_: (0,) * nd)


def row_loop(total, fn):
    step = 104 if total % 104 == 0 else 8

    def body(i, carry):
        fn(pl.ds(pl.multiple_of(i * step, 8), step))
        return carry

    lax.fori_loop(0, total // step, body, 0)


def norm_stats(v):
    center = v - jnp.mean(v, axis=-1, keepdims=True)
    rstd = lax.rsqrt(jnp.mean(center * center, axis=-1, keepdims=True) + EPS)
    return center, rstd


def col_sum(v):
    return jnp.sum(v, axis=0, keepdims=True)


def weight_ins(w, rows, nb, index):
    if isinstance(w, tuple):
        spec = pl.BlockSpec((4, rows // 8, nb), lambda k, ids: (0, 0, index(k)))
        return [(p, spec) for p in w]
    return [(w, pl.BlockSpec((rows, nb), lambda k, ids: (0, index(k))))]


def weight_scratch(w, rows, nb):
    return [pltpu.VMEM((rows, nb), bf16)] if isinstance(w, tuple) else []


def weight_ref(ids, refs, spare):
    if len(refs) == 1:
        return refs[0]
    rows = refs[0].shape[1]
    for q in range(4):
        for bit, ref in ((ids[IY], refs[0]), (1 - ids[IY], refs[1])):
            spare[pl.ds(pl.multiple_of((2 * q + bit) * rows, rows), rows), :] = ref[q]
    return spare


def nn_kernel(ids, xo, xt, *rest, n_w, epi, n_extra, n_out, flip):
    w = rest[:n_w]
    extra = rest[n_w : n_w + n_extra]
    outs = rest[n_w + n_extra : n_w + n_extra + n_out]
    xf = rest[n_w + n_extra + n_out]
    half = xo.shape[0]

    @pl.when(pl.program_id(0) == 0)
    def _():
        xf[0:half, :] = xo[...]
        xf[half:, :] = xt[...]
        if flip:
            nb = 256
            for at in range(0, xf.shape[1], nb):
                outs[-1][at : at + nb, :] = xf[:, at : at + nb].T

    w = weight_ref(ids, w, rest[-1])
    epi(ids, dot(xf[...], w[...]), extra, outs)


def nn_call(ids, xo, xt, w, col, steps, nb, epi, extra, outs, name, flip=False, us=5):
    half, width = xo.shape
    outs = list(outs)
    if flip:
        shape = (width, 2 * half)
        outs.append((shape, bf16, pl.BlockSpec(shape, lambda j, ids: (0, 0))))
    wi = weight_ins(w, width, nb, lambda j: col // nb + j)
    body = functools.partial(
        nn_kernel, n_w=len(wi), epi=epi, n_extra=len(extra), n_out=len(outs), flip=flip
    )
    return call(
        body,
        (steps,),
        [(xo, whole(xo)), (xt, whole(xt))] + wi + extra,
        outs,
        [pltpu.VMEM((2 * half, width), bf16)] + weight_scratch(w, width, nb),
        ids=ids,
        us=us,
        name=name,
    )


def epi_qkv(ids, y, extra, outs, *, base):
    (vec,) = extra
    j = pl.program_id(0)
    nb = y.shape[1]
    at = pl.multiple_of(ids[IC] * nb, nb)
    qb = vec[base + 2 : base + 3, pl.ds(at, nb)]
    vb = vec[base + 3 : base + 4, pl.ds(at, nb)]
    bias = jnp.where(j == 0, qb, jnp.where(j == 2, vb, 0.0))
    scale = jnp.where(j == 0, HD ** (-0.5), 1.0)
    outs[0][...] = ((y + bias) * scale).astype(bf16)


def gelu_parts(t):
    a = jnp.abs(t)
    k = 1.0 / (1.0 + 0.23164189 * a)
    e = jnp.exp(-0.5 * t * t)
    poly = k * (
        0.127414796 + k * (-0.142248368 + k * (0.7107068705 + k * (-0.7265760135 + k * 0.5307027145)))
    )
    tail = poly * e
    phi = jnp.where(t < 0, tail, 1.0 - tail)
    return phi, e * 0.3989422804014327


def epi_up(ids, y, extra, outs, *, base, own):
    (vec,) = extra
    j = pl.program_id(0)
    nb = y.shape[1]
    half = ids[IX] if own else 1 - ids[IX]
    row = base + 10 + 2 * ids[IC] + half
    bias = vec[pl.ds(row, 1), pl.ds(pl.multiple_of(j * nb, nb), nb)]
    u = y + bias
    phi, dens = gelu_parts(u)
    outs[0][...] = (u * phi).astype(bf16)
    outs[1][...] = (phi + u * dens).astype(bf16)


def epi_dact(ids, y, extra, outs):
    (gp,) = extra
    du = (y * gp[...].astype(f32)).astype(bf16)
    outs[0][...] = du
    outs[1][...] = col_sum(du.astype(f32))


def epi_plain(ids, y, extra, outs):
    outs[0][...] = y.astype(bf16)


def nt_kernel(ids, *rest, n_ws, epi, n_extra, n_out):
    n_in = sum(1 + n for n in n_ws)
    extra = rest[n_in : n_in + n_extra]
    outs = rest[n_in + n_extra : n_in + n_extra + n_out]
    acc = rest[n_in + n_extra + n_out]
    spares = rest[n_in + n_extra + n_out + 1 :]
    k = pl.program_id(0)
    nb = 256
    pairs = []
    at = 0
    for gi, n in enumerate(n_ws):
        spare = spares[gi] if spares else None
        pairs.append((rest[at], weight_ref(ids, rest[at + 1 : at + 1 + n], spare)))
        at += 1 + n

    def body(i, carry):
        cols = pl.ds(pl.multiple_of(i * nb, nb), nb)
        y = None
        for x, w in pairs:
            xv = x[...]
            v = dot(xv.reshape(xv.shape[-2:]), w[cols, :], NT)
            y = v if y is None else y + v

        @pl.when(k == 0)
        def _():
            acc[:, cols] = y

        @pl.when(k > 0)
        def _():
            acc[:, cols] += y

        return carry

    lax.fori_loop(0, acc.shape[1] // nb, body, 0)

    @pl.when(k == pl.num_programs(0) - 1)
    def _():
        epi(acc, extra, outs)


def nt_call(ids, groups, steps, kb, rows, wide, epi, extra, outs, name):
    ins, n_ws, scratch = [], [], [pltpu.VMEM((rows, wide), f32)]
    for x, xs, w, col in groups:
        ins.append((x, xs))
        wi = weight_ins(w, wide, kb, lambda k, c=col // kb: c + k)
        ins += wi
        n_ws.append(len(wi))
        scratch += weight_scratch(w, wide, kb)
    body = functools.partial(
        nt_kernel, n_ws=tuple(n_ws), epi=epi, n_extra=len(extra), n_out=len(outs)
    )
    return call(body, (steps,), ins + extra, outs, scratch, ids=ids, us=6, name=name)


def epi_send(acc, extra, outs):
    row_loop(acc.shape[0], lambda r: outs[0].__setitem__((r, slice(None)), acc[r, :].astype(bf16)))


def epi_proj(acc, extra, outs, *, base):
    recv, res, vec = extra
    mid_ref, branch_ref, h_ref = outs

    def fn(r):
        branch = acc[r, :] + recv[r, :].astype(f32) + vec[base + 4 : base + 5, :]
        mid = res[r, :].astype(f32) + vec[base + 5 : base + 6, :] * branch
        mid_ref[r, :] = mid
        branch_ref[r, :] = branch.astype(bf16)
        center, rstd = norm_stats(mid)
        h_ref[r, :] = (
            center * rstd * vec[base + 6 : base + 7, :] + vec[base + 7 : base + 8, :]
        ).astype(bf16)

    row_loop(acc.shape[0], fn)


def epi_down(acc, extra, outs, *, base, nxt):
    recv, mid, vec = extra
    out_ref, down_ref, h_ref = outs

    def fn(r):
        down = acc[r, :] + recv[r, :].astype(f32) + vec[base + 8 : base + 9, :]
        down_ref[r, :] = down.astype(bf16)
        res = mid[r, :] + vec[base + 9 : base + 10, :] * down
        out_ref[r, :] = res
        center, rstd = norm_stats(res)
        h_ref[r, :] = (
            center * rstd * vec[nxt : nxt + 1, :] + vec[nxt + 1 : nxt + 2, :]
        ).astype(bf16)

    row_loop(acc.shape[0], fn)


def epi_down_last(acc, extra, outs, *, base):
    recv, mid, vec, cot = extra
    out_ref, dd_ref, sums = outs
    sums[...] = jnp.zeros_like(sums)

    def fn(r):
        down = acc[r, :] + recv[r, :].astype(f32) + vec[base + 8 : base + 9, :]
        scale = vec[base + 9 : base + 10, :]
        out_ref[r, :] = mid[r, :] + scale * down
        g = cot[r, :].astype(f32)
        dd = (g * scale).astype(bf16)
        dd_ref[r, :] = dd
        sums[0:1, :] += col_sum(g * down)
        sums[1:2, :] += col_sum(dd.astype(f32))

    row_loop(acc.shape[0], fn)


def norm_back(grad, values, gain):
    center, rstd = norm_stats(values)
    n = center * rstd
    e = grad * gain
    me = jnp.mean(e, axis=-1, keepdims=True)
    men = jnp.mean(e * n, axis=-1, keepdims=True)
    return n, rstd * (e - me - n * men)


def epi_dh2(acc, extra, outs, *, base):
    recv, mid, g_in, branch, vec = extra
    dm_ref, db_ref, sums = outs
    sums[...] = jnp.zeros_like(sums)

    def fn(r):
        dh = acc[r, :] + recv[r, :].astype(f32)
        n, back = norm_back(dh, mid[r, :], vec[base + 6 : base + 7, :])
        dm = g_in[r, :].astype(f32) + back
        dm_ref[r, :] = dm
        db = (dm * vec[base + 5 : base + 6, :]).astype(bf16)
        db_ref[r, :] = db
        sums[0:1, :] += col_sum(dh * n)
        sums[1:2, :] += col_sum(dh)
        sums[2:3, :] += col_sum(dm * branch[r, :].astype(f32))
        sums[3:4, :] += col_sum(db.astype(f32))

    row_loop(acc.shape[0], fn)


def epi_dh1(acc, extra, outs, *, base, prev):
    if prev is None:
        recv, res, dm, vec = extra
        g_ref, sums = outs
    else:
        recv, res, dm, vec, down = extra
        g_ref, dd_ref, sums, dsums = outs
        dsums[...] = jnp.zeros_like(dsums)
    sums[...] = jnp.zeros_like(sums)

    def fn(r):
        dh = acc[r, :] + recv[r, :].astype(f32)
        n, back = norm_back(dh, res[r, :].astype(f32), vec[base : base + 1, :])
        g = dm[r, :] + back
        g_ref[r, :] = g
        sums[0:1, :] += col_sum(dh * n)
        sums[1:2, :] += col_sum(dh)
        if prev is not None:
            dd = (g * vec[prev + 9 : prev + 10, :]).astype(bf16)
            dd_ref[r, :] = dd
            dsums[0:1, :] += col_sum(g * down[r, :].astype(f32))
            dsums[1:2, :] += col_sum(dd.astype(f32))

    row_loop(acc.shape[0], fn)


def dw_kernel(ids, a_t, b, *rest, n_add, n_old, flat):
    y = dot(a_t[...], b[...].reshape(b.shape[-2:]))
    if n_add:
        y = y + rest[0][...].astype(f32)
    rest = rest[n_add + n_old :]
    if flat:
        rest[0][...] = y.astype(bf16)
        return
    keep, send, acc = rest
    acc[...] = y
    rows = keep.shape[1]
    for q in range(4):
        for bit, out in ((ids[IY], keep), (1 - ids[IY], send)):
            at = pl.multiple_of((2 * q + bit) * rows, rows)
            out[q] = acc[pl.ds(at, rows), :].astype(bf16)


def dw_call(ids, a_t, b, bspec, n, adds, name, flat=False, total=None, col=0, old=()):
    wide, tokens = a_t.shape
    nb = 256

    def cols(at):
        return pl.BlockSpec((wide, nb), lambda j, ids: (0, at // nb + j))

    if flat:
        outs = [((wide, total), bf16, cols(col))]
        scratch = []
    else:
        ospec = pl.BlockSpec((4, wide // 8, nb), lambda j, ids: (0, 0, col // nb + j))
        outs = [((4, wide // 8, total), bf16, ospec)] * 2
        scratch = [pltpu.VMEM((wide, nb), f32)]
    ins = [(a_t, whole(a_t)), (b, bspec)] + [(a, cols(at)) for a, at in adds]
    n_in = 1 + len(ins)
    ins += [(a, pl.BlockSpec(memory_space=pl.ANY)) for a in old]
    return call(
        functools.partial(dw_kernel, n_add=len(adds), n_old=len(old), flat=flat),
        (n // nb,),
        ins,
        outs,
        scratch,
        ids=ids,
        aliases={n_in + i: i for i in range(len(old))},
        name=name,
    )


def chunks_of(length):
    return [(s, min(256, length - s)) for s in range(0, length, 256)]


def head_lanes(rows, h):
    lane = lax.broadcasted_iota(jnp.int32, (rows, 2 * HD), 1)
    return (lane // HD) == h, lane == (1 - h) * HD


def attn_fwd_kernel(q_ref, k_ref, v_ref, mb_ref, o_ref, wide_ref, lse_ref):
    h = pl.program_id(0) % 2
    length = q_ref.shape[0]
    mine, mark = head_lanes(length, h)
    k0 = jnp.where(mine, k_ref[...].astype(f32), jnp.where(mark, mb_ref[...], 0.0)).astype(bf16)
    v_t = jnp.where(mine, v_ref[...].astype(f32), 1.0).astype(bf16).T
    for start, size in chunks_of(length):
        rows = pl.ds(start, size)
        mine_c, mark_c = head_lanes(size, h)
        q0 = jnp.where(mine_c, q_ref[rows, :].astype(f32), jnp.where(mark_c, 1.0, 0.0)).astype(bf16)
        s = dot(k0, q0, NT)
        top = jnp.max(s, axis=0, keepdims=True)
        p = jnp.exp(s - top).astype(bf16)
        o_t = dot(v_t, p)
        total = jnp.where(h == 0, o_t[HD : HD + 1, :], o_t[0:1, :])
        o = (o_t * (1.0 / total)).T
        o = jnp.where(mine_c, o, wide_ref[rows, :])
        wide_ref[rows, :] = o
        o_ref[rows, :] = o.astype(bf16)
        lse_ref[0, :, rows] = top + jnp.log(total)


def attn_fwd(qkv, mb):
    length, wide = qkv.shape
    pairs = wide // 3 // (2 * HD)
    blk = lambda off: pl.BlockSpec((length, 2 * HD), lambda g: (0, off + g // 2))
    return call(
        attn_fwd_kernel,
        (2 * pairs,),
        [(qkv, blk(0)), (qkv, blk(pairs)), (qkv, blk(2 * pairs)), (mb, whole(mb))],
        [
            ((length, wide // 3), bf16, blk(0)),
            ((length, wide // 3), f32, blk(0)),
            ((2 * pairs, 1, length), f32, pl.BlockSpec((1, 1, length), lambda g: (g, 0, 0))),
        ],
        us=30,
        name="attn_fwd",
    )


def attn_bwd_kernel(q_ref, k_ref, v_ref, do_ref, o_ref, mb_ref, lse_ref, g_ref, sums, dk_acc, dv_acc):
    h = pl.program_id(0) % 2
    length = q_ref.shape[0]
    mine, mark = head_lanes(length, h)
    kf = k_ref[...].astype(f32)
    k0 = jnp.where(mine, kf, jnp.where(mark, mb_ref[...], 0.0)).astype(bf16)
    k_t = k_ref[...].T
    v0 = jnp.where(mine, v_ref[...].astype(f32), 0.0).astype(bf16)
    for ci, (start, size) in enumerate(chunks_of(length)):
        rows = pl.ds(start, size)
        mine_c, mark_c = head_lanes(size, h)
        q = q_ref[rows, :]
        q0 = jnp.where(mine_c, q.astype(f32), jnp.where(mark_c, 1.0, 0.0)).astype(bf16)
        do = do_ref[rows, :]
        inner = jnp.where(mine_c, do.astype(f32) * o_ref[rows, :], 0.0)
        delta = jnp.sum(inner.T, axis=0, keepdims=True)
        p = jnp.exp(dot(k0, q0, NT) - lse_ref[0, :, rows])
        ds = (p * (dot(v0, do, NT) - delta)).astype(bf16)
        dv = dot(p.astype(bf16), do)
        dk = dot(ds, q)
        if ci == 0:
            dv_acc[...] = dv
            dk_acc[...] = dk
        else:
            dv_acc[...] += dv
            dk_acc[...] += dk
        dq = dot(k_t, ds).T * HD ** (-0.5)
        g_ref[0, rows, :] = jnp.where(mine_c, dq, g_ref[0, rows, :].astype(f32)).astype(bf16)
    g_ref[1] = jnp.where(mine, dk_acc[...], g_ref[1].astype(f32)).astype(bf16)
    g_ref[2] = jnp.where(mine, dv_acc[...], g_ref[2].astype(f32)).astype(bf16)

    @pl.when(h == 1)
    def _():
        sums[0] = col_sum(g_ref[0].astype(f32))
        sums[1] = col_sum(g_ref[2].astype(f32))


def attn_bwd(qkv, d_mixed, mixed, mb, lse):
    length, wide = qkv.shape
    pairs = wide // 3 // (2 * HD)
    blk = lambda off: pl.BlockSpec((length, 2 * HD), lambda g: (0, off + g // 2))
    return call(
        attn_bwd_kernel,
        (2 * pairs,),
        [
            (qkv, blk(0)),
            (qkv, blk(pairs)),
            (qkv, blk(2 * pairs)),
            (d_mixed, blk(0)),
            (mixed, blk(0)),
            (mb, whole(mb)),
            (lse, pl.BlockSpec((1, 1, length), lambda g: (g, 0, 0))),
        ],
        [
            (
                (3, length, wide // 3),
                bf16,
                pl.BlockSpec((3, length, 2 * HD), lambda g: (0, 0, g // 2)),
            ),
            ((2, 1, wide // 3), f32, pl.BlockSpec((2, 1, 2 * HD), lambda g: (0, 0, g // 2))),
        ],
        [pltpu.VMEM((length, 2 * HD), f32), pltpu.VMEM((length, 2 * HD), f32)],
        us=30,
        name="attn_bwd",
    )


def ln_kernel(x, vec, out, *, base):
    def fn(r):
        center, rstd = norm_stats(x[r, :].astype(f32))
        out[r, :] = (center * rstd * vec[base : base + 1, :] + vec[base + 1 : base + 2, :]).astype(bf16)

    row_loop(x.shape[0], fn)


def ln_call(x, vec, base):
    return call(
        functools.partial(ln_kernel, base=base),
        (1,),
        [(x, whole(x)), (vec, whole(vec))],
        [(x.shape, bf16, whole(x))],
        name="ln",
    )[0]


def vec_grad_kernel(ids, ln1, qv, ln2, down, ub_o, ub_t, out):
    out[...] = jnp.zeros_like(out)
    n = qv.shape[2]
    at = pl.multiple_of(ids[IC] * n, n)
    out[0:2, :] = ln1[0:2, :]
    out[2:3, pl.ds(at, n)] = qv[0]
    out[3:4, pl.ds(at, n)] = qv[1]
    out[4:5, :] = ln2[3:4, :]
    out[5:6, :] = ln2[2:3, :]
    out[6:8, :] = ln2[0:2, :]
    out[8:9, :] = down[1:2, :]
    out[9:10, :] = down[0:1, :]
    row = 10 + 2 * ids[IC]
    out[pl.ds(row + ids[IX], 1), :] = ub_o[...]
    out[pl.ds(row + 1 - ids[IX], 1), :] = ub_t[...]


def adam_math(w, g, m, v, rate, decay):
    m1 = B1 * m + (1.0 - B1) * g
    v1 = B2 * v + (1.0 - B2) * g * g
    step = -rate * (
        (m1 * (1.0 / (1.0 - B1**STEPS))) / (jnp.sqrt(v1 * (1.0 / (1.0 - B2**STEPS))) + ADAM_EPS)
        + decay * w.astype(f32)
    )
    return step, m1, v1


def adam_kernel(ids, *rest, pick, n_g, n_old):
    gs = rest[:n_g]
    w, m, v = rest[n_g : n_g + 3]
    g_out, s_out, m_out, v_out = rest[n_g + 3 + n_old :]
    g = pick(ids, pl.program_id(0), gs)
    step, m1, v1 = adam_math(w[0], g, m[0], v[0], RATE_M, DECAY)
    g_out[0] = g
    s_out[0] = step
    m_out[0] = m1
    v_out[0] = v1


def pick_attn(ids, b, gs):
    own, oth = [g[...].astype(f32) for g in gs]
    return jnp.where((b % 2) == ids[IC], own, oth)


def pick_mlp(ids, b, gs):
    own, oth = gs
    core = ((b // 2) % 2) == ids[IC]
    at = pl.ds(((b % 2) + ids[IX]) % 2, 1)
    return jnp.where(core, own[at][0].astype(f32), oth[at][0].astype(f32))


def adam_call(ids, layer, gs, gspecs, w, m, v, nb, pick, old, name):
    spec = pl.BlockSpec((1, w.shape[1], nb), lambda b, ids: (layer, 0, b))
    ins = list(zip(gs, gspecs)) + [(w, spec), (m, spec), (v, spec)]
    n_in = len(ins) + 1
    ins += [(o, pl.BlockSpec(memory_space=pl.ANY)) for o in old]
    return call(
        functools.partial(adam_kernel, pick=pick, n_g=len(gs), n_old=len(old)),
        (w.shape[2] // nb,),
        ins,
        [(w.shape, f32, spec)] * 4,
        ids=ids,
        aliases={n_in + i: i for i in range(len(old))},
        name=name,
    )


def copy_kernel(ids, a, out):
    out[...] = a[0]


def pick_columns(ids, a, layer, nb, steps, index, name):
    rows = a.shape[1]
    return call(
        copy_kernel,
        (steps,),
        [(a, pl.BlockSpec((1, rows, nb), lambda j, ids: (layer, 0, index(j, ids))))],
        [((rows, nb * steps), bf16, pl.BlockSpec((rows, nb), lambda j, ids: (0, j)))],
        ids=ids,
        name=name,
    )[0]


SWAP = [(0, 1), (1, 0)]


def swap_core(a):
    return lax.ppermute(a, "seq", SWAP)


def swap_x(a):
    return lax.ppermute(a, "dp", SWAP)


def swap_bit(a, bit):
    return lax.ppermute(a, "fsdp", [(i, i ^ bit) for i in range(8)])


def merge_kernel(ids, own, recv, out, *, bit):
    mine = pl.program_id(1) == ids[bit]

    @pl.when(mine)
    def _():
        out[0] = own[...]

    @pl.when(jnp.logical_not(mine))
    def _():
        out[0] = recv[...]


def merge(ids, own, recv, bit):
    a, b, n = own.shape
    ins = pl.BlockSpec((1, b, n), lambda i, j, ids: (i, 0, 0))
    (out,) = call(
        functools.partial(merge_kernel, bit=bit),
        (a, 2),
        [(own, ins), (recv, ins)],
        [((a, 2, b, n), own.dtype, pl.BlockSpec((1, 1, b, n), lambda i, j, ids: (i, j, 0, 0)))],
        ids=ids,
        name="merge",
    )
    return out.reshape(2 * a, b, n)


def merge_z_kernel(ids, *rest):
    out = rest[-1]
    z = 2 * ids[IZ1] + ids[IZ0]
    for k, part in enumerate(rest[:-1]):
        out[pl.ds((z - k + 4) % 4, 1)] = part[...][None]


def gather_z(ids, own):
    parts = [own] + [
        lax.ppermute(own, "fsdp", [(i, (i + 2 * k) % 8) for i in range(8)]) for k in range(1, 4)
    ]
    b, n = own.shape
    nb = 512
    ins = pl.BlockSpec((b, nb), lambda j, ids: (0, j))
    return call(
        merge_z_kernel,
        (n // nb,),
        [(p, ins) for p in parts],
        [((4, b, n), own.dtype, pl.BlockSpec((4, b, nb), lambda j, ids: (0, 0, j)))],
        ids=ids,
        name="merge_z",
    )[0]


def fold_kernel(ids, keep, recv, keep_out, send_out, *, bit):
    for a in range(keep_out.shape[0]):
        for b, out in ((ids[bit], keep_out), (1 - ids[bit], send_out)):
            at = 2 * a + b
            v = keep[pl.ds(at, 1)].astype(f32) + recv[pl.ds(at, 1)].astype(f32)
            out[a] = v[0].astype(bf16)


def fold(ids, keep, recv, bit):
    a, b, n = keep.shape
    nb = 512
    ins = pl.BlockSpec((a, b, nb), lambda j, ids: (0, 0, j))
    outs = pl.BlockSpec((a // 2, b, nb), lambda j, ids: (0, 0, j))
    return call(
        functools.partial(fold_kernel, bit=bit),
        (n // nb,),
        [(keep, ins), (recv, ins)],
        [((a // 2, b, n), bf16, outs)] * 2,
        ids=ids,
        name="fold",
    )


def apart(go, fn, *args):
    def empty(*args):
        return jax.tree.map(lambda v: jnp.zeros(v.shape, v.dtype), jax.eval_shape(fn, *args))

    return lax.cond(go, fn, empty, *args)


def tie(*arrays):
    return lax.optimization_barrier(arrays)


def local(
    tokens_in,
    key_mask,
    attn_weights,
    mlp_weights,
    vectors,
    cotangent,
    first_attn,
    second_attn,
    first_mlp,
    second_mlp,
    first_vec,
    second_vec,
):
    layers, shard, _ = attn_weights.shape
    n_fsdp = lax.axis_size("fsdp")
    staged = n_fsdp == 8
    c = lax.axis_index("seq")
    x = lax.axis_index("dp")
    f = lax.axis_index("fsdp")
    ids = jnp.stack([f // 4 % 2, f // 2 % 2, f % 2, c, x]).astype(jnp.int32)

    tokens = tokens_in[0]
    go = key_mask[0, 0] >= 0
    cot = cotangent[0]
    half, wide = tokens.shape
    length = 2 * half
    group = wide // 2
    bias = jnp.where(key_mask[0] > 0, 0.0, -1e30).astype(f32).reshape(2, half)
    bias = jnp.where(c == 0, bias, bias[::-1]).reshape(length, 1)
    mb = jnp.broadcast_to(bias, (length, 2 * HD))

    pa = [
        pick_columns(ids, attn_weights, l, group, 4, lambda j, ids: 2 * j + ids[IC], "pick_a")
        for l in range(layers)
    ]
    pm = [
        pick_columns(
            ids, mlp_weights, l, wide, 2, lambda j, ids: 4 * j + 2 * ids[IC] + ids[IX], "pick_m"
        )
        for l in range(layers)
    ]
    pv = vectors.reshape(1, layers * ROWS, -1)
    def line(p, bits):
        for bit, at in bits:
            p = merge(ids, p, swap_bit(p, bit), at)
        return p

    Z1, Z0, Y = (4, IZ1), (2, IZ0), (1, IY)
    if staged:
        vec = line(pv, (Z1, Z0, Y))
    else:
        vec = lax.all_gather(pv, "fsdp", axis=0, tiled=True)
    vec = vec.transpose(1, 0, 2).reshape(layers * ROWS, -1).astype(f32)

    h_own = ln_call(tokens, vec, 0)
    h_own, *pm = tie(h_own, *pm)
    h_oth = apart(go, swap_core, h_own)
    wa, wm = [None] * layers, [None] * layers
    for l in range(layers):
        a = pa[l]
        if staged and l == 1:
            a, z4 = tie(a, z4)
        wa[l] = lax.all_gather(a, "fsdp", axis=0, tiled=True)
        if not staged:
            w = lax.all_gather(pm[l], "fsdp", axis=0, tiled=True)
            wm[l] = [w, swap_x(w)]
        elif l == 0:
            z4 = gather_z(ids, pm[0])

    vspec = pl.BlockSpec(vec.shape, lambda *_: (0, 0))
    V = (vec, vspec)
    own = pl.BlockSpec((half, wide), lambda *_: (0, 0))

    def xs(row, kb):
        return pl.BlockSpec((half, kb), lambda k, ids: (row, k))

    def fixed(shape):
        return pl.BlockSpec(shape, lambda *_: (0,) * len(shape))

    KB = 512
    nb = 256
    colspec = pl.BlockSpec((length, nb), lambda j, ids: (0, j))
    send_out = [((half, wide), bf16, own)]
    res = tokens
    saved = []
    for l in range(layers):
        base = l * ROWS
        if staged and l == 0:
            h_oth, z4 = tie(h_oth, z4)
            y0 = swap_bit(z4, 1)
            far_a = swap_x(z4)
            pm_next, _ = tie(pm[1][None], z4)
        if staged and l == 1:
            z4 = m_four
        qkv, h_t = nn_call(
            ids, h_own, h_oth, wa[l], 0, 3, group, functools.partial(epi_qkv, base=base), [V],
            [((length, 3 * group), bf16, pl.BlockSpec((length, group), lambda j, ids: (0, j)))],
            "qkv", flip=True,
        )
        if staged and l == 1:
            qkv, y1, far_a = tie(qkv, y1, far_a)
            far_b = swap_x(y1)
        mixed, mixed_wide, lse = attn_fwd(qkv, mb)
        if staged and l == 0:
            m_recv = swap_bit(pm_next, 4)
            mixed, y0, far_a, m_recv = tie(mixed, y0, far_a, m_recv)
            wm[0] = [(z4, y0), (far_a, swap_x(y0))]
            m_two = merge(ids, pm_next, m_recv, IZ1)
            m_recv = swap_bit(m_two, 2)
        if staged and l == 1:
            wm[1] = [(z4, y1), (far_a, far_b)]

        def proj_pair(mixed, w, res, vec):
            def proj(row, epi, extra, outs):
                return nt_call(
                    ids, [(mixed, xs(row, KB), w, 3 * group)], group // KB, KB, half, wide, epi,
                    extra, outs, "proj",
                )

            (part,) = proj(1, epi_send, [], send_out)
            mid, branch, h2_own = proj(
                0, functools.partial(epi_proj, base=base),
                [(swap_core(part), own), (res, own), (vec, vspec)],
                [((half, wide), f32, own), ((half, wide), bf16, own), ((half, wide), bf16, own)],
            )
            return mid, branch, h2_own, swap_core(h2_own)

        mid, branch, h2_own, h2_oth = apart(go, proj_pair, mixed, wa[l], res, vec)
        act, gp = [], []
        for i in (0, 1):
            if i == 1:
                h2_own, act[0] = tie(h2_own, act[0])
            got = nn_call(
                ids, h2_own, h2_oth, wm[l][i], 0, wide // nb, nb,
                functools.partial(epi_up, base=base, own=i == 0), [V],
                [((length, wide), bf16, colspec)] * 2, "up", flip=i == 0,
            )
            act.append(got[0])
            gp.append(got[1])
            if i == 0:
                h2_t = got[2]

        if staged and l == 0:
            act[0], act[1], m_recv = tie(act[0], act[1], m_recv)
            m_four = merge(ids, m_two, m_recv, IZ0)
            y1 = swap_bit(m_four, 1)
            far_a = swap_x(m_four)
        last = l == layers - 1

        def down_pair(act, wm, mid, vec, cot):
            def down(row, epi, extra, outs):
                return nt_call(
                    ids, [(act[i], xs(row, KB), wm[i], wide) for i in (0, 1)],
                    wide // KB, KB, half, wide, epi, extra, outs, "down",
                )

            (part,) = down(1, epi_send, [], send_out)
            recv = swap_core(part)
            if last:
                out, dd_own, dsums = down(
                    0, functools.partial(epi_down_last, base=base),
                    [(recv, own), (mid, own), (vec, vspec), (cot, own)],
                    [((half, wide), f32, own), ((half, wide), bf16, own), ((2, wide), f32, fixed((2, wide)))],
                )
                return out, dd_own, dsums, swap_core(dd_own)
            out, down_out, h_next = down(
                0, functools.partial(epi_down, base=base, nxt=base + ROWS),
                [(recv, own), (mid, own), (vec, vspec)],
                [((half, wide), f32, own), ((half, wide), bf16, own), ((half, wide), bf16, own)],
            )
            return out, h_next, down_out, swap_core(h_next)

        out, next_own, extra_out, next_oth = apart(go, down_pair, act, wm[l], mid, vec, cot)
        if last:
            dd_own, dd_oth, dsums, down_out = next_own, next_oth, extra_out, None
        else:
            down_out = extra_out
        saved.append((res, h_t, qkv, mixed, mixed_wide, lse, mid, branch, h2_t, act, gp, down_out))
        if not last:
            res, h_own, h_oth = out, next_own, next_oth
    tokens_out = out

    g = cot
    old_a, old_m = [], []
    gvecs = [None] * layers
    pend = {}

    def step_y(key, parts):
        if staged:
            pend[key] = (parts[0], swap_bit(parts[1], 1))
        else:
            pend[key] = lax.psum_scatter(parts[0], "fsdp", scatter_dimension=0, tiled=True)

    def tied(key, other):
        other, pend[key] = tie(other, pend[key])
        return other

    def step_z0(key):
        keep, send = fold(ids, *pend[key], IZ0)
        pend[key] = (keep, swap_bit(send, 2))

    def step_z1(key):
        keep, send = fold(ids, *pend[key], IZ1)
        pend[key] = (keep, swap_bit(send, 4))

    def step_end(key):
        keep, recv = pend[key]
        return keep[0].astype(f32) + recv[0].astype(f32)

    for l in reversed(range(layers)):
        base = l * ROWS
        lower = l > 0
        split = not lower
        flat = lower or not staged
        res, h_t, qkv, mixed, mixed_wide, lse, mid, branch, h2_t, act, gp, _ = saved[l]
        du, ub = [None, None], [None, None]
        for i in (1, 0):
            got = nn_call(
                ids, dd_own, dd_oth, wm[l][i], wide, wide // nb, nb, epi_dact,
                [(gp[i], colspec)],
                [((length, wide), bf16, colspec), ((1, wide), f32, pl.BlockSpec((1, nb), lambda j, ids: (0, j)))],
                "dact", flip=i == 1,
            )
            du[i], ub[i] = got[:2]
            if i == 1:
                dd_t = got[2]
                if split:
                    far = []
                    for a_t, b in ((h2_t, du[1]), (dd_t, act[1])):
                        far += dw_call(ids, a_t, b, colspec, wide, [], "dw_far", flat=True, total=wide)
                    dd_own, *_ = tie(dd_own, *far)
                    far = [swap_x(v) for v in far]
        if not split:
            d_m = ()
            for n, (a_t, b) in enumerate(((h2_t, du[0]), (dd_t, act[0]), (h2_t, du[1]), (dd_t, act[1]))):
                d_m = dw_call(
                    ids, a_t, b, colspec, wide, [], "dw_mlp", flat=True, total=4 * wide, col=n * wide, old=d_m
                )
            du[0], d_m = tie(du[0], d_m[0])
            pend[("m", l)] = lax.psum_scatter(d_m, "fsdp", scatter_dimension=0, tiled=True)

        def dh2_pair(du, wm, mid, g, branch, vec):
            def dh2(row, epi, extra, outs):
                return nt_call(
                    ids, [(du[i], xs(row, KB), wm[i], 0) for i in (0, 1)],
                    wide // KB, KB, half, wide, epi, extra, outs, "dh2",
                )

            (part,) = dh2(1, epi_send, [], send_out)
            dm, db_own, sums2 = dh2(
                0, functools.partial(epi_dh2, base=base),
                [(swap_core(part), own), (mid, own), (g, own), (branch, own), (vec, vspec)],
                [((half, wide), f32, own), ((half, wide), bf16, own), ((4, wide), f32, fixed((4, wide)))],
            )
            return dm, db_own, sums2, swap_core(db_own)

        dm, db_own, sums2, db_oth = apart(go, dh2_pair, du, wm[l], mid, g, branch, vec)
        if split:
            db_oth, pend[("m", l + 1)] = tie(db_oth, pend[("m", l + 1)])
            d_up, _ = tie(pend[("a", l + 1)], pend[("m", l + 1)])
            pend[("a", l + 1)] = lax.psum_scatter(d_up, "fsdp", scatter_dimension=0, tiled=True)
        d_mixed, db_t = nn_call(
            ids, db_own, db_oth, wa[l], 3 * group, group // nb, nb, epi_plain, [],
            [((length, group), bf16, colspec)], "dmixed", flip=True,
        )
        d_a = dw_call(
            ids, db_t, mixed, colspec, group, [], "dw_p", flat=flat, total=4 * group, col=3 * group
        )
        d_mixed, d_a = tie(d_mixed, d_a)
        d_qkv, qv = attn_bwd(qkv, d_mixed, mixed_wide, mb, lse)
        qspec = pl.BlockSpec((1, length, nb), lambda j, ids: (j * nb // group, 0, j % (group // nb)))
        d_a = dw_call(
            ids, h_t, d_qkv, qspec, 3 * group, [], "dw_qkv", flat=flat, total=4 * group, old=d_a
        )
        d_qkv, d_a = tie(d_qkv, d_a)
        if not split:
            pend[("a", l)] = d_a[0]
        else:
            step_y("a", d_a)
        down_below = saved[l - 1][-1] if lower else None

        def dh1_pair(d_qkv, w, res, dm, vec, down_below):
            def dh1(row, epi, extra, outs):
                spec = pl.BlockSpec((1, half, group), lambda k, ids: (k, row, 0))
                return nt_call(ids, [(d_qkv, spec, w, 0)], 3, group, half, wide, epi, extra, outs, "dh1")

            (part,) = dh1(1, epi_send, [], send_out)
            extra = [(swap_core(part), own), (res, own), (dm, own), (vec, vspec)]
            outs = [((half, wide), f32, own), ((2, wide), f32, fixed((2, wide)))]
            if lower:
                extra.append((down_below, own))
                outs[1:1] = [((half, wide), bf16, own)]
                outs.append(((2, wide), f32, fixed((2, wide))))
            got = dh1(0, functools.partial(epi_dh1, base=base, prev=base - ROWS if lower else None), extra, outs)
            return got, swap_core(got[1]) if lower else ()

        got, below_oth = apart(go, dh1_pair, d_qkv, wa[l], res, dm, vec, down_below)
        if split:
            g_first, *far = tie(got[0], *far)
            near = ()
            for n, (a_t, b) in enumerate(((h2_t, du[0]), (dd_t, act[0]))):
                near = dw_call(
                    ids, a_t, b, colspec, wide, [(far[n], 0)], "dw_near", flat=flat,
                    total=2 * wide, col=n * wide, old=near,
                )
            g_first, near = tie(g_first, near)
            step_y("m", near)
            if staged:
                pend["a"], _ = tie(pend["a"], near)
                step_z0("a")
            got = [g_first] + list(got[1:])
        sums1 = got[2] if lower else got[1]

        (gvecs[l],) = call(
            vec_grad_kernel,
            (1,),
            [(a, whole(a)) for a in (sums1, qv, sums2, dsums, ub[0], ub[1])],
            [((16, wide), f32, fixed((16, wide)))],
            ids=ids,
            name="vec_grad",
        )
        g = got[0]
        if lower:
            dd_own, dd_oth, dsums = got[1], below_oth, got[3]
    grad_tokens = g

    gv = jnp.stack(gvecs)
    if staged:
        gv, _ = tie(gv, pend["a"])
        gv = gv + swap_core(gv)
        gv = gv + swap_x(gv)
        for bit in (1, 2, 4):
            gv = gv + swap_bit(gv, bit)
    else:
        gv = lax.psum(gv, ("dp", "fsdp", "seq"))

    for l in reversed(range(layers)):
        if l == 0 and staged:
            pend["m"], pend["a"], old_a, old_m = tie(
                pend["m"], pend["a"], tuple(old_a), tuple(old_m)
            )
            step_z0("m")
            step_z1("m")
            g_a = step_end("a").astype(bf16)
        elif l == 0:
            g_a, g_m = pend["a"], pend["m"]
        else:
            g_a, g_m = pend[("a", l)], pend[("m", l)]
        g_a = (g_a.astype(f32) + swap_x(g_a).astype(f32)).astype(bf16)
        g_at = swap_core(g_a)
        aspec = pl.BlockSpec((shard, group), lambda b, ids: (0, b // 2))
        old_a = adam_call(
            ids, l, [g_a, g_at], [aspec, aspec], attn_weights, first_attn, second_attn,
            group, pick_attn, old_a, "adam_attn",
        )
        if l > 0:
            late, _ = tie(g_m, far[1])
            r_m = swap_x(late)
            if staged:
                r_m, pend["a"] = tie(r_m, pend["a"])
                step_z1("a")
            n = 2 * wide
            g_m = jnp.stack(
                [
                    (g_m[:, :n].astype(f32) + r_m[:, n:].astype(f32)).astype(bf16),
                    (g_m[:, n:].astype(f32) + r_m[:, :n].astype(f32)).astype(bf16),
                ]
            )
        else:
            if staged:
                pend["m"], old_a, gv = tie(pend["m"], tuple(old_a), gv)
                g_m = step_end("m").astype(bf16)
            g_m = jnp.stack([g_m, swap_x(g_m)])
        g_mt = swap_core(g_m)
        mspec = pl.BlockSpec((2, shard, wide), lambda b, ids: (0, 0, b // 4))
        old_m = adam_call(
            ids, l, [g_m, g_mt], [mspec] * 2, mlp_weights, first_mlp, second_mlp,
            wide, pick_mlp, old_m, "adam_mlp",
        )

    gv = lax.dynamic_slice_in_dim(gv, f * (wide // n_fsdp), wide // n_fsdp, axis=2)
    gv = gv[:, :ROWS]
    step_v, one_v, two_v = adam_math(vectors, gv, first_vec, second_vec, RATE_V, 0.0)

    return (
        tokens_out[None],
        grad_tokens[None],
        old_a[0],
        old_m[0],
        gv,
        old_a[1],
        old_m[1],
        step_v,
        old_a[2],
        old_a[3],
        old_m[2],
        old_m[3],
        one_v,
        two_v,
    )


def solution(mesh):
    tok = P(("dp", "fsdp"), "seq", None)
    mat = P(None, "fsdp", None)
    vec = P(None, None, "fsdp")
    return jax.shard_map(
        local,
        mesh=mesh,
        in_specs=(tok, P(("dp", "fsdp"), None), mat, mat, vec, tok, mat, mat, mat, mat, vec, vec),
        out_specs=(tok, tok, mat, mat, vec, mat, mat, vec, mat, mat, mat, mat, vec, vec),
        check_vma=False,
    )
```
